256 devices in a mesh: dp: 32 (over z, x_hi, core), tensor: 8 (over y, x_lo).
Axes of the slice: x: 4 (x_hi: 2, x_lo: 2; x = x_hi * 2 + x_lo), y: 4, z: 8, core: 2. Of those that a mesh axis runs over, the one named last changes fastest.
Arguments:
- grads: bfloat16 [32, 40, 128, 4096], P('dp', None, None, 'tensor'), may hold values from -6 to 6
- owner: int32 [40], replicated, may hold values from 0 to 31, as said below
- momentum: float32 [32, 2, 128, 4096], P('dp', None, None, 'tensor'), may hold values from -6 to 6, as said below
Outputs:
- update: bfloat16 [40, 128, 4096], P(None, None, 'tensor')
- new_momentum: float32 [32, 2, 128, 4096], P('dp', None, None, 'tensor')
The draws below stay inside these ranges and needn't reach their ends.
Inputs may be any that keep to these rules, and one draw needn't show every extreme that they name: Every owner holds at least one matrix and no owner holds more than 2; some owner holds exactly 2. Slot s of owner p holds the momentum of the matrix of slot_rank s among those that owner p holds; slots beyond an owner's count hold values that are carried over.
All inputs are finite; a program needn't handle non-finite values.
Results may differ from the reference program's by a relative error of at most 0.03.
Values may be sent and summed in bfloat16 or wider, within the bound.
A program may use at most 64 MiB of HBM per device.

```python
import math
import jax
import jax.numpy as jnp
from jax import lax

R = 128
D = 4096
EXTRA = 8
SLOTS = 2
ITERS = 5
OWNERS = 32
MATS = 40


def draw_owner(key, part):
    folded = jax.random.fold_in(key, 11)
    key_owner, key_extra, key_order = jax.random.split(folded, 3)
    owner_perm = jax.random.permutation(key_owner, OWNERS).astype(jnp.int32)
    base = jnp.arange(OWNERS, dtype=jnp.int32) * SLOTS
    forced = jnp.arange(1, SLOTS, dtype=jnp.int32)
    others = jnp.arange((OWNERS - 1) * (SLOTS - 1), dtype=jnp.int32)
    candidates = (1 + others // (SLOTS - 1)) * SLOTS + 1 + others % (SLOTS - 1)
    chosen = jax.random.permutation(key_extra, candidates)[:EXTRA - (SLOTS - 1)].astype(jnp.int32)
    picks = jnp.concatenate([base, forced, chosen])
    holders = owner_perm[picks // SLOTS]
    shuffle = jax.random.permutation(key_order, MATS).astype(jnp.int32)
    return holders[shuffle].astype(jnp.int32)


def draw_momentum(key, part):
    folded = jax.random.fold_in(key, 23)
    key_value, key_row, key_col = jax.random.split(folded, 3)
    entries = jax.random.truncated_normal(key_value, -3.0, 3.0, (OWNERS, SLOTS, R, D), jnp.float32)
    log_top = math.log(10.0)
    row_scale = jnp.exp(jax.random.uniform(key_row, (OWNERS, SLOTS, R, 1), jnp.float32, 0.0, log_top))
    col_scale = jnp.exp(jax.random.uniform(key_col, (1, 1, 1, D), jnp.float32, 0.0, log_top))
    return 0.02 * entries * row_scale * col_scale


def level_of(key, shape, cuts, low, largest):
    gain = 1.0
    for position, blocks in cuts:
        heights = jax.random.uniform(jax.random.fold_in(jax.random.fold_in(key, 6), position), (blocks,), jnp.float32, low / len(cuts), largest / len(cuts))
        gain = gain * jnp.repeat(jnp.exp(heights), shape[position] // blocks).reshape((-1,) + (1,) * (len(shape) - 1 - position))
    return gain


def bell_draw(rng, dims, deviation, bound, pieces=(), kind=jnp.bfloat16):
    drawn = deviation * jax.random.normal(rng, dims, jnp.float32)
    if pieces:
        drawn = drawn * level_of(rng, dims, pieces, -0.22, 0.18)
    return jnp.clip(drawn, -bound, bound).astype(kind)


def setup_inputs(seed: int = 0) -> dict:
    key_list = jax.random.split(jax.random.key(seed), 4)
    grads = bell_draw(key_list[0], (OWNERS, MATS, R, D), 1.0, 6.0, ((0, 32), (3, 8)))
    owner = draw_owner(jax.random.fold_in(key_list[3], 71), 0)
    momentum = draw_momentum(jax.random.fold_in(key_list[3], 71), 0)
    return dict(grads=grads, owner=owner, momentum=momentum)


COEF_A = 3.4445
COEF_B = -4.775
COEF_C = 2.0315
EPSILON = 1e-07
DECAY = 0.95

def orthogonalize(rounded):
    squares = jnp.sum(jnp.square(rounded.astype(jnp.float32)))
    iterate = (rounded.astype(jnp.float32) / (jnp.sqrt(squares) + EPSILON)).astype(jnp.bfloat16)
    factor = 0.2 * math.sqrt(max(R, D))
    following = None
    for step in range(ITERS):
        gram = jnp.dot(iterate, iterate.T, preferred_element_type=jnp.float32).astype(jnp.bfloat16)
        gram = lax.optimization_barrier(gram)
        polynomial = (COEF_B * gram.astype(jnp.float32) + COEF_C * jnp.dot(gram, gram, preferred_element_type=jnp.float32)).astype(jnp.bfloat16)
        following = COEF_A * iterate.astype(jnp.float32) + jnp.dot(polynomial, iterate, preferred_element_type=jnp.float32)
        if step + 1 < ITERS:
            iterate = following.astype(jnp.bfloat16)
    return (factor * following).astype(jnp.bfloat16)

def reference(grads, owner, momentum):
    positions = jnp.arange(MATS, dtype=jnp.int32)
    same_owner = owner[:, None] == owner[None, :]
    earlier = positions[None, :] < positions[:, None]
    slot_rank = lax.optimization_barrier(jnp.sum((same_owner & earlier).astype(jnp.int32), axis=1)).astype(jnp.int32)

    def one_matrix(matrix_id):
        replicas = lax.dynamic_index_in_dim(grads, matrix_id, 1, keepdims=False)
        mean_grad = lax.optimization_barrier(jnp.sum(replicas.astype(jnp.float32), axis=0)) / OWNERS
        previous = momentum[owner[matrix_id], slot_rank[matrix_id]]
        following = DECAY * previous + mean_grad
        rounded = (mean_grad + DECAY * following).astype(jnp.bfloat16)
        return (orthogonalize(rounded), following)
    update, momentum_next = lax.map(one_matrix, positions)
    new_momentum = momentum.at[owner, slot_rank].set(momentum_next)
    return (update, new_momentum)
```

```python
import functools
import math

import jax
import jax.numpy as jnp
from jax import lax
from jax.experimental import pallas as pl
from jax.experimental.pallas import tpu as pltpu
from jax.sharding import PartitionSpec as P

D = 4096
ITERS = 5
COEF_A = 3.4445
COEF_B = -4.775
COEF_C = 2.0315
EPSILON = 1e-07
DECAY = 0.95

DEPTH = 8
F32 = jnp.float32
BF16 = jnp.bfloat16

GAIN = 1.0 + DECAY

SECOND, HOLDER, PLACE = 32, 40, 48


def table_kernel(owner_ref, out_ref):
    owners = SECOND

    @pl.loop(0, owners)
    def _(p):
        out_ref[p] = -1

    def body(m, count):
        who = owner_ref[m]
        seen = out_ref[who] >= 0

        @pl.when(seen)
        def _():
            out_ref[SECOND + count] = m
            out_ref[HOLDER + count] = who

        @pl.when(jnp.logical_not(seen))
        def _():
            out_ref[who] = m

        out_ref[PLACE + m] = jnp.where(seen, owners + count, who)
        return count + seen.astype(jnp.int32)

    lax.fori_loop(0, owner_ref.shape[0], body, jnp.int32(0))


def order_kernel(place_ref, in_ref, out_ref, held, sems):
    count = out_ref.shape[0]

    def fetch(m):
        return pltpu.make_async_copy(in_ref.at[place_ref[PLACE + m]], held.at[m], sems.at[0, m])

    def store(m):
        return pltpu.make_async_copy(held.at[m], out_ref.at[m], sems.at[1, m])

    for m in range(count):
        fetch(m).start()
    for m in range(count):
        fetch(m).wait()
        store(m).start()
    for m in range(count):
        store(m).wait()


def split(a):
    high = a.astype(BF16)
    return high, (a - high.astype(F32)).astype(BF16)


def dot(a, b):
    return jnp.dot(a, b, preferred_element_type=F32)


def product(a, b):
    return dot(a[0], b[0]) + (dot(a[0], b[1]) + dot(a[1], b[0]))


def polynomials(grams, factor):
    size = grams[0].shape[0]
    row = lax.broadcasted_iota(jnp.int32, (size, size), 0)
    col = lax.broadcasted_iota(jnp.int32, (size, size), 1)
    diagonal = row == col
    eye = jnp.where(diagonal, 1.0, 0.0).astype(F32)
    scales, now = [], []
    for gram in grams:
        total = jnp.sum(jnp.where(diagonal, gram, 0.0), keepdims=True)
        scale = 1.0 / (jnp.sqrt(total) + EPSILON)
        scales.append(scale)
        now.append((gram * scale) * scale)
    totals = [None] * len(grams)
    for step in range(ITERS):
        parts = [split(g) for g in now]
        squares = [product(g, g) for g in parts]
        polys = [COEF_A * eye + COEF_B * g + COEF_C * s for g, s in zip(now, squares)]
        poly_parts = [split(p) for p in polys]
        if step + 1 < ITERS:
            once = [product(p, g) for p, g in zip(poly_parts, parts)]
        if step == 0:
            totals = polys
        else:
            totals = [product(p, split(q)) for p, q in zip(poly_parts, totals)]
        if step + 1 < ITERS:
            now = [product(p, split(o)) for p, o in zip(poly_parts, once)]
    return [q * (scale * factor) for q, scale in zip(totals, scales)]


def step_kernel(
    table, grads, momentum, gathered, new_momentum,
    gv, mv, pstage, precv, xstage, xrecv, zstage, zrecv, tstage, trecv, total, rows16,
    names, gpart, grecv, gsum, gall,
    load_sem, psend, precv_sem, xsend, xrecv_sem, zsend, zrecv_sem, tsend, trecv_sem,
    gsend, grecv_sem, nz, nx, npair, nrecv, az, ax, apair, arecv,
):
    me = lax.axis_index("dp")
    t = lax.axis_index("tensor")
    tensors = lax.axis_size("tensor")
    owners = lax.axis_size("dp")
    c = lax.rem(me, 2)
    h = lax.rem(me // 2, 2)
    z = me // 4
    rows, cols = gv.shape[1], gv.shape[2]
    half = rows // 2
    strip = rows // tensors
    TOP, BOTTOM = pl.ds(0, half), pl.ds(half, half)
    factor = 0.2 * math.sqrt(max(rows, D))
    turn = 1 - 2 * c

    def at(k):
        return lax.rem(z + k + 2 * DEPTH, DEPTH)

    def dp_of(zz, hh, cc):
        return 4 * zz + 2 * hh + cc

    def remote(src, dst, send, recv, dp=None, tensor=None):
        return pltpu.make_async_remote_copy(
            src_ref=src, dst_ref=dst, send_sem=send, recv_sem=recv,
            device_id={"dp": me if dp is None else dp, "tensor": t if tensor is None else tensor},
            device_id_type=pl.DeviceIdType.MESH,
        )

    partner = dp_of(z, h, 1 - c)
    across = dp_of(z, 1 - h, c)
    on0, on1 = c == 0, c == 1
    holder = jnp.logical_and(c == 0, h == 0)

    def toward(k):
        return dp_of(at(k), h, c)

    matrices = gv.shape[0]
    loads = load_sem.shape[0] - 1
    span = matrices // loads
    for i in range(loads):
        pltpu.make_async_copy(
            grads.at[0, pl.ds(i * span, span)], gv.at[pl.ds(i * span, span)], load_sem.at[i]
        ).start()
    pltpu.make_async_copy(momentum.at[0], mv, load_sem.at[loads]).start()

    barrier = pltpu.get_barrier_semaphore()
    for peer in (partner, across, toward(1), toward(-1)):
        pl.semaphore_signal(
            barrier, inc=1, device_id={"dp": peer, "tensor": t}, device_id_type=pl.DeviceIdType.MESH
        )
    for i in range(1, tensors):
        pl.semaphore_signal(
            barrier, inc=1, device_id={"dp": me, "tensor": lax.rem(t + i, tensors)},
            device_id_type=pl.DeviceIdType.MESH,
        )
    pl.semaphore_wait(barrier, 4 + tensors - 1)

    for i in range(loads):
        pltpu.make_async_copy(
            grads.at[0, pl.ds(i * span, span)], gv.at[pl.ds(i * span, span)], load_sem.at[i]
        ).wait()
    pltpu.make_async_copy(momentum.at[0], mv, load_sem.at[loads]).wait()

    order = (4, 3, -3, 2, -2, 1, -1, 0)
    fold = DECAY * DECAY * owners / GAIN

    def extra(zz, part):
        mine = jnp.where(table[HOLDER + zz] == me, fold, 0.0).astype(F32)
        return gv[table[SECOND + zz], part, :].astype(F32) + mine * mv[1, part, :]

    def pair(slot):
        return remote(pstage.at[slot], precv.at[slot], psend.at[slot], precv_sem.at[slot], dp=partner)

    for k in order:
        zz = at(k)
        for hh in range(2):
            pstage[2 * zz + hh] = gv[table[dp_of(zz, hh, 1 - c)]]
            pair(2 * zz + hh).start()

        @pl.when(on1)
        def _():
            for part in (TOP, BOTTOM):
                pstage[16 + zz, part, :] = extra(zz, part).astype(BF16)
            pair(16 + zz).start()

    def own(zz, hh, part):
        return gv[table[dp_of(zz, hh, c)], part, :].astype(F32) + precv[2 * zz + hh, part, :].astype(F32)

    def contribution(u, zz):
        if u == 0:
            return own(zz, h, TOP)
        if u == 1:
            return own(zz, 1 - h, TOP)
        if u == 2:
            return own(zz, h, BOTTOM) + xrecv[zz].astype(F32)
        part = TOP if u == 3 else BOTTOM
        return extra(zz, part) + precv[16 + zz, part, :].astype(F32)

    signs = (1, -1, turn, 1, -1)

    def zcopy(u, slot, src, k):
        return remote(src, zrecv.at[u, slot], zsend.at[u, slot], zrecv_sem.at[u, slot], dp=toward(k))

    def zwait(u, slot):
        zcopy(u, slot, zrecv.at[u, slot], 0 + signs[u]).wait_recv()

    def first(u, place, slot, k, away):
        zstage[u, place] = contribution(u, at(k)).astype(BF16)
        zcopy(u, slot, zstage.at[u, place], away).start()

    def passed(u, slot, k, away):
        zwait(u, slot)
        zrecv[u, slot] = (zrecv[u, slot].astype(F32) + contribution(u, at(k))).astype(BF16)
        zcopy(u, slot + 1, zrecv.at[u, slot], away).start()

    def zstep(u, distance):
        sign = signs[u]
        if distance == 4:
            first(u, 0, 0, 4 * sign, sign)
        elif distance == 3:
            first(u, 1, 4, -3 * sign, -sign)
            passed(u, 0, 3 * sign, sign)
        elif distance == 2:
            passed(u, 1, 2 * sign, sign)
            passed(u, 4, -2 * sign, -sign)
        else:
            passed(u, 2, sign, sign)
            passed(u, 5, -sign, -sign)

    def zlast(u):
        zwait(u, 3)
        zwait(u, 6)
        return contribution(u, z) + (zrecv[u, 3].astype(F32) + zrecv[u, 6].astype(F32))

    def xcopy(zz):
        return remote(xstage.at[zz], xrecv.at[zz], xsend.at[zz], xrecv_sem.at[zz], dp=across)

    def xstep(k):
        zz = at(k)
        for hh in range(2):
            pair(2 * zz + hh).wait_recv()
        xstage[zz] = own(zz, 1 - h, BOTTOM).astype(BF16)
        xcopy(zz).start()

        @pl.when(on0)
        def _():
            pair(16 + zz).wait_recv()

    def group(distance):
        zstep(0, distance)
        zstep(1, distance)

        @pl.when(on0)
        def _():
            zstep(3, distance)
            zstep(4, distance)

    xstep(4)
    zstep(0, 4)
    zstep(1, 4)

    @pl.when(on0)
    def _():
        zstep(3, 4)
        zstep(4, 4)

    for k in order[1:]:
        xstep(k)
    group(3)
    xcopy(at(4)).wait_recv()
    zstep(2, 4)
    group(2)
    for k in (3, -3):
        xcopy(at(k)).wait_recv()
    zstep(2, 3)
    group(1)
    for k in (2, -2):
        xcopy(at(k)).wait_recv()
    zstep(2, 2)

    def tcopy(i):
        return remote(tstage.at[i], trecv.at[i], tsend.at[i], trecv_sem.at[i], dp=across)

    tstage[0] = zlast(1).astype(BF16)
    tcopy(0).start()

    @pl.when(on0)
    def _():
        for i, part in ((1, TOP), (2, BOTTOM)):
            partial = zlast(2 + i)

            @pl.when(h == 1)
            def _():
                tstage[i] = partial.astype(BF16)
                tcopy(i).start()

            @pl.when(h == 0)
            def _():
                total[1, part, :] = partial

    total[0, TOP, :] = zlast(0)
    for k in (1, -1):
        xcopy(at(k)).wait_recv()
    zstep(2, 1)
    xcopy(z).wait_recv()
    total[0, BOTTOM, :] = zlast(2)
    tcopy(0).wait_recv()
    total[0, TOP, :] += trecv[0].astype(F32)

    mean = total[0] * (1.0 / owners)
    following = DECAY * mv[0] + mean
    new_momentum[0, 0] = following
    rows16[0] = (mean + DECAY * following).astype(BF16)

    def gram(j):
        gpart[j] = lax.dot_general(
            rows16[j], rows16[j], (((1,), (1,)), ((), ())), preferred_element_type=F32
        )

    def strip_of(i):
        return pl.ds(pl.multiple_of(i * strip, strip), strip)

    def scatter(j, i, back=False):
        peer = lax.rem(t + i, tensors)
        slot = peer if back else t
        return remote(
            gpart.at[j, strip_of(peer)], grecv.at[j, slot], gsend.at[0, j, i], grecv_sem.at[0, j, slot],
            tensor=peer,
        )

    def spread(j, i, back=False):
        peer = lax.rem(t + i, tensors)
        slot = peer if back else t
        return remote(
            gsum.at[j], gall.at[j, strip_of(slot)], gsend.at[1, j, i], grecv_sem.at[1, j, slot],
            tensor=peer,
        )

    gram(0)
    for i in range(1, tensors):
        scatter(0, i).start()

    def block(ref, zz, u):
        if u == 0:
            return ref.at[dp_of(zz, h, c), TOP], 2 * dp_of(zz, h, c)
        if u == 1:
            return ref.at[dp_of(zz, 1 - h, c), TOP], 2 * dp_of(zz, 1 - h, c)
        if u == 2:
            return ref.at[dp_of(zz, h, c), BOTTOM], 2 * dp_of(zz, h, c) + 1
        base = owners if ref is gathered else 0
        return ref.at[base + zz, TOP if u == 3 else BOTTOM], 2 * (base + zz) + (u - 3)

    def sets(ref):
        return (nz, nx, npair, nrecv) if ref is names else (az, ax, apair, arecv)

    def zhop(ref, u, zz, slot, away):
        z_sem, _, _, recv = sets(ref)
        view, index = block(ref, zz, u)
        return remote(view, view, z_sem.at[u - 3 if ref is names else u, slot], recv.at[index], dp=toward(away))

    def arrival(ref, u, zz):
        z_sem, _, _, recv = sets(ref)
        view, index = block(ref, zz, u)
        return remote(view, view, z_sem.at[0, 0], recv.at[index], dp=across)

    def xhop(ref, view, index, slot):
        _, x_sem, _, recv = sets(ref)
        return remote(view, view, x_sem.at[slot], recv.at[index], dp=across)

    def phop(ref, view, index, slot):
        _, _, p_sem, recv = sets(ref)
        return remote(view, view, p_sem.at[slot], recv.at[index], dp=partner)

    def local(zz, u):
        if u == 0:
            return 4 * zz + 2 * h
        if u == 1:
            return 4 * zz + 2 * (1 - h)
        if u == 2:
            return 4 * zz + 2 * h + 1
        return 32 + 2 * zz + (u - 3)

    def pass_on(ref, u, zz):
        view, index = block(ref, zz, u)
        slot = 2 * zz + u - 3 if ref is names else local(zz, u)
        phop(ref, view, index, slot).start()

    def begin(ref, u):
        sign = signs[u]
        zhop(ref, u, z, 0, sign).start()
        zhop(ref, u, z, 4, -sign).start()
        pass_on(ref, u, z)

    def hop(ref, u, distance):
        sign = signs[u]
        zz = at(-sign * distance)
        arrival(ref, u, zz).wait_recv()
        if distance < 4:
            zhop(ref, u, zz, distance, sign).start()
        pass_on(ref, u, zz)
        done = [zz]
        if distance < 4:
            zz = at(sign * distance)
            arrival(ref, u, zz).wait_recv()
            if distance < 3:
                zhop(ref, u, zz, 4 + distance, -sign).start()
            pass_on(ref, u, zz)
            done.append(zz)
        return done

    @pl.when(holder)
    def _():
        for i, part in ((1, TOP), (2, BOTTOM)):
            tcopy(i).wait_recv()
            value = (total[1, part, :] + trecv[i].astype(F32)) * (GAIN / owners)
            rows16[1, part, :] = value.astype(BF16)
            names[z, part, :] = value.astype(BF16)
        gram(1)
        for i in range(1, tensors):
            scatter(1, i).start()
        for u in (3, 4):
            view, index = block(names, z, u)
            xhop(names, view, index, u - 3).start()
            begin(names, u)

    def reduce_strip(j):
        acc = gpart[j, strip_of(t)]
        for i in range(1, tensors):
            scatter(j, i, back=True).wait_recv()
            acc = acc + grecv[j, lax.rem(t + i, tensors)]
        gsum[j] = acc
        gall[j, strip_of(t)] = acc
        for i in range(1, tensors):
            spread(j, i).start()

    reduce_strip(0)

    @pl.when(holder)
    def _():
        reduce_strip(1)

    @pl.when(jnp.logical_and(on0, h == 1))
    def _():
        for u in (3, 4):
            arrival(names, u, z).wait_recv()
            begin(names, u)

    def finish(js):
        results = polynomials([gall[j] for j in js], factor)
        for j, q in zip(js, results):
            high, low = split(q)
            value = dot(high, rows16[j]) + dot(low, rows16[j])
            gathered[me if j == 0 else owners + z] = value.astype(BF16)

    for i in range(1, tensors):
        spread(0, i, back=True).wait_recv()

    @pl.when(holder)
    def _():
        for i in range(1, tensors):
            spread(1, i, back=True).wait_recv()
        finish((0, 1))

    @pl.when(jnp.logical_not(holder))
    def _():
        finish((0,))

    view, index = block(gathered, z, 0)
    xhop(gathered, view, index, 8).start()
    begin(gathered, 2)
    begin(gathered, 0)
    view, index = block(gathered, z, 2)
    xhop(gathered, view, index, z).start()

    @pl.when(holder)
    def _():
        for u in (3, 4):
            view, index = block(gathered, z, u)
            xhop(gathered, view, index, 6 + u).start()
            begin(gathered, u)

    @pl.when(on0)
    def _():
        for u in (3, 4):
            hop(names, u, 1)

    arrival(gathered, 1, z).wait_recv()
    begin(gathered, 1)

    @pl.when(jnp.logical_and(on0, h == 1))
    def _():
        for u in (3, 4):
            arrival(gathered, u, z).wait_recv()
            begin(gathered, u)

    def from_across(zz):
        index = dp_of(zz, 1 - h, c)
        view = gathered.at[index, BOTTOM]
        xhop(gathered, view, 2 * index + 1, 0).wait_recv()
        phop(gathered, view, 2 * index + 1, 4 * zz + 2 * (1 - h) + 1).start()

    waiting = [z]
    for distance in (1, 2, 3, 4):
        arrived = hop(gathered, 2, distance)
        for zz in arrived:
            view, index = block(gathered, zz, 2)
            xhop(gathered, view, index, zz).start()
        if distance > 1:
            @pl.when(on0)
            def _():
                for u in (3, 4):
                    hop(names, u, distance)
        hop(gathered, 0, distance)
        hop(gathered, 1, distance)

        @pl.when(on0)
        def _():
            for u in (3, 4):
                hop(gathered, u, distance)

        for zz in waiting:
            from_across(zz)
        waiting = arrived
    for zz in waiting:
        from_across(zz)

    def from_partner(ref, view, index):
        phop(ref, view, index, 0).wait_recv()

    @pl.when(on1)
    def _():
        for zz in range(DEPTH):
            for u in (3, 4):
                view, index = block(names, zz, u)
                from_partner(names, view, index)

    has = jnp.float32(0.0)
    which = jnp.int32(0)
    for e in range(DEPTH):
        hit = table[HOLDER + e] == me
        has = jnp.where(hit, 1.0, has)
        which = jnp.where(hit, e, which)
    old = mv[1]
    mean = names[which].astype(F32) * (1.0 / GAIN) - (DECAY * DECAY / GAIN) * old
    new_momentum[0, 1] = old + has * ((DECAY * old + mean) - old)

    for zz in range(DEPTH):
        for hh in range(2):
            for i, part in enumerate((TOP, BOTTOM)):
                index = dp_of(zz, hh, 1 - c)
                from_partner(gathered, gathered.at[index, part], 2 * index + i)

    @pl.when(on1)
    def _():
        for zz in range(DEPTH):
            for u in (3, 4):
                view, index = block(gathered, zz, u)
                from_partner(gathered, view, index)

    for slot in range(16):
        pair(slot).wait_send()
    for zz in range(DEPTH):
        xcopy(zz).wait_send()
    tcopy(0).wait_send()
    for u in range(3):
        for slot in range(7):
            zcopy(u, slot, zrecv.at[u, slot], 1).wait_send()
    for i in range(1, tensors):
        scatter(0, i).wait_send()
        spread(0, i).wait_send()

    def sent(sem):
        view = zrecv.at[0, 0]
        remote(view, view, sem, zrecv_sem.at[0, 0], dp=across).wait_send()

    for u in range(3):
        for slot in range(7):
            sent(az.at[u, slot])
    for i in range(9):
        sent(ax.at[i])
    for i in range(32):
        sent(apair.at[i])

    @pl.when(on1)
    def _():
        for zz in range(DEPTH):
            pair(16 + zz).wait_send()

    @pl.when(on0)
    def _():
        for i in range(2):
            for slot in range(7):
                zcopy(3 + i, slot, zrecv.at[3 + i, slot], 1).wait_send()
                sent(az.at[3 + i, slot])
                sent(nz.at[i, slot])
        for i in range(16):
            sent(apair.at[32 + i])
            sent(npair.at[i])

        @pl.when(h == 1)
        def _():
            for i in (1, 2):
                tcopy(i).wait_send()

    @pl.when(holder)
    def _():
        for i in range(1, tensors):
            scatter(1, i).wait_send()
            spread(1, i).wait_send()
        for i in range(2):
            sent(ax.at[9 + i])
            sent(nx.at[i])


def per_device(grads, owner, momentum):
    tensors = lax.axis_size("tensor")
    matrices, rows, cols = grads.shape[1:]
    slots = momentum.shape[1]
    half = rows // 2
    table = pl.pallas_call(
        table_kernel,
        out_shape=jax.ShapeDtypeStruct((128,), jnp.int32),
        in_specs=[pl.BlockSpec(memory_space=pltpu.SMEM)],
        out_specs=pl.BlockSpec(memory_space=pltpu.SMEM),
        name="tables",
    )(owner)
    dma = pltpu.SemaphoreType.DMA
    gathered, new_momentum = pl.pallas_call(
        step_kernel,
        out_shape=(
            jax.ShapeDtypeStruct((matrices, rows, cols), BF16),
            jax.ShapeDtypeStruct(momentum.shape, F32),
        ),
        in_specs=[
            pl.BlockSpec(memory_space=pltpu.SMEM),
            pl.BlockSpec(memory_space=pl.ANY),
            pl.BlockSpec(memory_space=pl.ANY),
        ],
        out_specs=(
            pl.BlockSpec(memory_space=pltpu.VMEM),
            pl.BlockSpec(memory_space=pltpu.VMEM),
        ),
        scratch_shapes=[
            pltpu.VMEM((matrices, rows, cols), BF16),
            pltpu.VMEM((slots, rows, cols), F32),
            pltpu.VMEM((24, rows, cols), BF16),
            pltpu.VMEM((24, rows, cols), BF16),
            pltpu.VMEM((DEPTH, half, cols), BF16),
            pltpu.VMEM((DEPTH, half, cols), BF16),
            pltpu.VMEM((5, 2, half, cols), BF16),
            pltpu.VMEM((5, 7, half, cols), BF16),
            pltpu.VMEM((3, half, cols), BF16),
            pltpu.VMEM((3, half, cols), BF16),
            pltpu.VMEM((2, rows, cols), F32),
            pltpu.VMEM((2, rows, cols), BF16),
            pltpu.VMEM((DEPTH, rows, cols), BF16),
            pltpu.VMEM((2, rows, rows), F32),
            pltpu.VMEM((2, tensors, rows // tensors, rows), F32),
            pltpu.VMEM((2, rows // tensors, rows), F32),
            pltpu.VMEM((2, rows, rows), F32),
            dma((9,)),
            dma((24,)), dma((24,)),
            dma((DEPTH,)), dma((DEPTH,)),
            dma((5, 7)), dma((5, 7)),
            dma((3,)), dma((3,)),
            dma((2, 2, tensors)), dma((2, 2, tensors)),
            dma((2, 7)), dma((2,)), dma((16,)), dma((16,)),
            dma((5, 7)), dma((11,)), dma((48,)), dma((2 * matrices,)),
        ],
        compiler_params=pltpu.CompilerParams(collective_id=0, has_side_effects=True),
        name="step",
    )(table, grads, momentum)
    update = pl.pallas_call(
        order_kernel,
        out_shape=jax.ShapeDtypeStruct((matrices, rows, cols), BF16),
        in_specs=[
            pl.BlockSpec(memory_space=pltpu.SMEM),
            pl.BlockSpec(memory_space=pl.ANY),
        ],
        out_specs=pl.BlockSpec(memory_space=pl.ANY),
        scratch_shapes=[pltpu.VMEM((matrices, rows, cols), BF16), dma((2, matrices))],
        name="order",
    )(table, gathered)
    return update, new_momentum


def solution(mesh):
    in_specs = (P("dp", None, None, "tensor"), P(), P("dp", None, None, "tensor"))
    out_specs = (P(None, None, "tensor"), P("dp", None, None, "tensor"))
    return jax.shard_map(
        per_device, mesh=mesh, in_specs=in_specs, out_specs=out_specs, check_vma=False
    )
```

```python
import functools
import math

import jax
import jax.numpy as jnp
from jax import lax
from jax.experimental import pallas as pl
from jax.experimental.pallas import tpu as pltpu
from jax.sharding import PartitionSpec as P

D = 4096
ITERS = 5
COEF_A = 3.4445
COEF_B = -4.775
COEF_C = 2.0315
EPSILON = 1e-07
DECAY = 0.95

DEPTH = 8
F32 = jnp.float32
BF16 = jnp.bfloat16

GAIN = 1.0 + DECAY

FIRST, SECOND, HOLDER, PLACE = range(4)


def tables(owner, owners, out):
    count = owner.shape[1]

    def grid(shape, dim):
        return lax.broadcasted_iota(jnp.int32, shape, dim)

    def column(row):
        size = row.shape[1]
        square = (size, size)
        kept = jnp.where(grid(square, 0) == grid(square, 1), jnp.broadcast_to(row, square), 0)
        return jnp.sum(kept, axis=1, keepdims=True)

    held = column(owner) == grid((count, owners), 1)
    which = grid((count, owners), 0)
    first = jnp.min(jnp.where(held, which, count - 1), axis=0, keepdims=True)
    last = jnp.max(jnp.where(held, which, -1), axis=0, keepdims=True)
    first_c, last_c = column(first), column(last)
    two = jnp.where(last > first, 1, 0)
    two_c = column(two)
    square = (owners, owners)
    rank = jnp.sum(
        jnp.where(grid(square, 0) < grid(square, 1), jnp.broadcast_to(two_c, square), 0),
        axis=0, keepdims=True,
    )
    rank_c = column(rank)
    eighth = (owners, DEPTH)
    chosen = jnp.logical_and(
        jnp.broadcast_to(rank_c, eighth) == grid(eighth, 1), jnp.broadcast_to(two_c, eighth) > 0
    )
    second = jnp.sum(jnp.where(chosen, jnp.broadcast_to(last_c, eighth), 0), axis=0, keepdims=True)
    holder = jnp.sum(jnp.where(chosen, grid(eighth, 0), 0), axis=0, keepdims=True)
    wide = (owners, count)
    spot = jnp.where(
        jnp.broadcast_to(first_c, wide) == grid(wide, 1), grid(wide, 0), owners + rank_c
    )
    place = jnp.sum(
        jnp.where(jnp.broadcast_to(owner, wide) == grid(wide, 0), spot, 0), axis=0, keepdims=True
    )
    out[FIRST, 0:owners] = first[0]
    out[SECOND, 0:DEPTH] = second[0]
    out[HOLDER, 0:DEPTH] = holder[0]
    out[PLACE, 0:count] = place[0]


def order_kernel(table, in_ref, momentum, out_ref, out_momentum, sems):
    count = out_ref.shape[0]

    def copy(m):
        return pltpu.make_async_copy(in_ref.at[table[PLACE, m]], out_ref.at[m], sems.at[m])

    rest = pltpu.make_async_copy(momentum, out_momentum, sems.at[count])
    for m in range(count):
        copy(m).start()
    rest.start()
    for m in range(count):
        copy(m).wait()
    rest.wait()


def split(a):
    high = a.astype(BF16)
    return high, (a - high.astype(F32)).astype(BF16)


def dot(a, b):
    return jnp.dot(a, b, preferred_element_type=F32)


def product(a, b):
    return dot(a[0], b[0]) + (dot(a[0], b[1]) + dot(a[1], b[0]))


def polynomials(grams, factor):
    size = grams[0].shape[0]
    row = lax.broadcasted_iota(jnp.int32, (size, size), 0)
    col = lax.broadcasted_iota(jnp.int32, (size, size), 1)
    diagonal = row == col
    eye = jnp.where(diagonal, 1.0, 0.0).astype(F32)
    scales, now = [], []
    for gram in grams:
        total = jnp.sum(jnp.where(diagonal, gram, 0.0), keepdims=True)
        scale = 1.0 / (jnp.sqrt(total) + EPSILON)
        scales.append(scale)
        now.append((gram * scale) * scale)
    totals = [None] * len(grams)
    for step in range(ITERS):
        parts = [split(g) for g in now]
        squares = [product(g, g) for g in parts]
        polys = [COEF_A * eye + COEF_B * g + COEF_C * s for g, s in zip(now, squares)]
        poly_parts = [split(p) for p in polys]
        if step + 1 < ITERS:
            once = [product(p, g) for p, g in zip(poly_parts, parts)]
        if step == 0:
            totals = polys
        else:
            totals = [product(p, split(q)) for p, q in zip(poly_parts, totals)]
        if step + 1 < ITERS:
            now = [product(p, split(o)) for p, o in zip(poly_parts, once)]
    return [q * (scale * factor) for q, scale in zip(totals, scales)]


def step_kernel(
    owner, grads, momentum, gathered, new_momentum, table_out,
    gv, mv, pstage, precv, xstage, xrecv, zstage, zrecv, tstage, trecv, total,
    nall, qall, gpart, grecv, gsum, gall, table, folded,
    load_sem, sent, precv_sem, xrecv_sem, zrecv_sem, trecv_sem, grecv_sem,
    arecv, parecv, qrecv, pqrecv,
):
    (s_pair, s_x, s_z, s_top, s_az, s_xtop, s_xbottom, s_xextra, s_passed, s_qz, s_qze, s_qx, s_qxe,
     s_qpassed) = (sent.at[i] for i in range(14))
    s_scatter, s_spread = (sent.at[14], sent.at[16]), (sent.at[15], sent.at[17])
    me = lax.axis_index("dp")
    t = lax.axis_index("tensor")
    tensors = lax.axis_size("tensor")
    owners = lax.axis_size("dp")
    c = lax.rem(me, 2)
    h = lax.rem(me // 2, 2)
    z = me // 4
    rows, cols = gv.shape[1], gv.shape[2]
    half = rows // 2
    strip = rows // tensors
    TOP, BOTTOM = pl.ds(0, half), pl.ds(half, half)
    factor = 0.2 * math.sqrt(max(rows, D))
    turn = 1 - 2 * c

    def at(k):
        return lax.rem(z + k + 2 * DEPTH, DEPTH)

    def dp_of(zz, hh, cc):
        return 4 * zz + 2 * hh + cc

    def remote(src, dst, send, recv, dp=None, tensor=None):
        return pltpu.make_async_remote_copy(
            src_ref=src, dst_ref=dst, send_sem=send, recv_sem=recv,
            device_id={"dp": me if dp is None else dp, "tensor": t if tensor is None else tensor},
            device_id_type=pl.DeviceIdType.MESH,
        )

    partner = dp_of(z, h, 1 - c)
    across = dp_of(z, 1 - h, c)
    on0, on1 = c == 0, c == 1
    holder = jnp.logical_and(c == 0, h == 0)

    def toward(k):
        return dp_of(at(k), h, c)
    matrices = gv.shape[0]
    loads = 8
    span = matrices // loads
    for i in range(loads):
        pltpu.make_async_copy(
            grads.at[0, pl.ds(i * span, span)], gv.at[pl.ds(i * span, span)], load_sem.at[0]
        ).start()
    momentum_load = pltpu.make_async_copy(momentum.at[0], mv, load_sem.at[1])
    momentum_load.start()

    barrier = pltpu.get_barrier_semaphore()
    for peer in (partner, across, toward(1), toward(-1)):
        pl.semaphore_signal(
            barrier, inc=1, device_id={"dp": peer, "tensor": t}, device_id_type=pl.DeviceIdType.MESH
        )
    for i in range(1, tensors):
        pl.semaphore_signal(
            barrier, inc=1, device_id={"dp": me, "tensor": lax.rem(t + i, tensors)},
            device_id_type=pl.DeviceIdType.MESH,
        )

    table_out[...] = jnp.zeros_like(table_out)
    tables(owner[...], owners, table_out)
    to_scalars = pltpu.make_async_copy(table_out, table, load_sem.at[2])
    to_scalars.start()
    pl.semaphore_wait(barrier, 4 + tensors - 1)
    momentum_load.wait()
    folded[...] = (mv[1] * (DECAY * DECAY * owners / GAIN)).astype(BF16)
    to_scalars.wait()
    pltpu.make_async_copy(grads.at[0], gv, load_sem.at[0]).wait()

    order = (4, 3, -3, 2, -2, 1, -1, 0)

    def chosen(row, i):
        return jnp.clip(table[row, i], 0, matrices - 1)

    def extra(zz, part):
        mine = jnp.where(table[HOLDER, zz] == me, 1.0, 0.0).astype(BF16)
        return gv[chosen(SECOND, zz), part, :] + mine * folded[part, :]

    def pair(slot, zz):
        return remote(pstage.at[slot], precv.at[slot], s_pair, precv_sem.at[zz], dp=partner)
    for k in order:
        zz = at(k)
        for hh in range(2):
            pstage[2 * zz + hh] = gv[chosen(FIRST, dp_of(zz, hh, 1 - c))]
            pair(2 * zz + hh, zz).start()

        @pl.when(on1)
        def _():
            for part in (TOP, BOTTOM):
                pstage[16 + zz, part, :] = extra(zz, part)
            pair(16 + zz, zz).start()

    def several(ref, send, recv, dp=partner):
        return remote(ref, ref, send, recv, dp=dp)

    def paired(*offsets):
        for k in offsets:
            for here, matrices in ((on0, 3), (on1, 2)):
                @pl.when(here)
                def _():
                    several(precv.at[pl.ds(0, matrices)], s_pair, precv_sem.at[at(k)]).wait_recv()

    def own(zz, hh, part):
        return gv[chosen(FIRST, dp_of(zz, hh, c)), part, :] + precv[2 * zz + hh, part, :]

    def contribution(u, zz):
        if u == 0:
            return own(zz, h, TOP)
        if u == 1:
            return own(zz, 1 - h, TOP)
        if u == 2:
            return own(zz, h, BOTTOM) + xrecv[zz]
        part = TOP if u == 3 else BOTTOM
        return extra(zz, part) + precv[16 + zz, part, :]

    signs = (1, -1, turn, 1, -1)

    def zcopy(u, slot, src, k):
        return remote(src, zrecv.at[u, slot], s_z, zrecv_sem.at[u, slot], dp=toward(k))

    def zwait(u, slot):
        zcopy(u, slot, zrecv.at[u, slot], signs[u]).wait_recv()

    def first(u, place, slot, k, away):
        zstage[u, place] = contribution(u, at(k))
        zcopy(u, slot, zstage.at[u, place], away).start()

    def passed(u, slot, k, away):
        zwait(u, slot)
        zrecv[u, slot] = zrecv[u, slot] + contribution(u, at(k))
        zcopy(u, slot + 1, zrecv.at[u, slot], away).start()

    def z4(u):
        first(u, 0, 0, 4 * signs[u], signs[u])

    def z3b(u):
        first(u, 1, 4, -3 * signs[u], -signs[u])

    def z3a(u):
        passed(u, 0, 3 * signs[u], signs[u])

    def z3(u):
        z3b(u)
        z3a(u)

    def z2(u):
        passed(u, 1, 2 * signs[u], signs[u])
        passed(u, 4, -2 * signs[u], -signs[u])

    def z1(u):
        passed(u, 2, signs[u], signs[u])
        passed(u, 5, -signs[u], -signs[u])

    def zlast(u):
        zwait(u, 3)
        zwait(u, 6)
        return contribution(u, z).astype(F32) + (zrecv[u, 3].astype(F32) + zrecv[u, 6].astype(F32))

    def xcopy(zz):
        return remote(xstage.at[zz], xrecv.at[zz], s_x, xrecv_sem.at[zz], dp=across)

    def xstep(*offsets):
        for k in offsets:
            zz = at(k)
            xstage[zz] = own(zz, 1 - h, BOTTOM)
            xcopy(zz).start()

    def crossed(*offsets):
        for k in offsets:
            xcopy(at(k)).wait_recv()

    def every(step):
        step(0)
        step(1)

        @pl.when(on0)
        def _():
            step(3)
            step(4)
    paired(4)
    every(z4)
    xstep(4)
    paired(3, -3)
    every(z3b)
    xstep(3, -3)
    every(z3a)
    paired(2, -2)
    xstep(2, -2)
    paired(1, -1)
    xstep(1, -1)
    crossed(4)
    z4(2)
    every(z2)
    paired(0)
    xstep(0)
    crossed(3, -3)
    z3(2)
    every(z1)
    crossed(2, -2)
    z2(2)

    def tcopy(i):
        return remote(
            tstage.at[i], trecv.at[i], s_top, trecv_sem.at[0 if i == 0 else 1], dp=across
        )
    tstage[0] = zlast(1).astype(BF16)
    tcopy(0).start()

    @pl.when(on0)
    def _():
        for i, part in ((1, TOP), (2, BOTTOM)):
            partial = zlast(2 + i)

            @pl.when(h == 1)
            def _():
                tstage[i] = partial.astype(BF16)
                tcopy(i).start()

            @pl.when(h == 0)
            def _():
                total[1, part, :] = partial

    total[0, TOP, :] = zlast(0)
    crossed(1, -1)
    z1(2)

    def block(zz, u):
        if u < 3:
            hh = 1 - h if u == 1 else h
            lower = 1 if u == 2 else 0
            return nall.at[dp_of(zz, hh, c), BOTTOM if lower else TOP], 4 * zz + 2 * hh + lower
        return nall.at[owners + zz, TOP if u == 3 else BOTTOM], 4 * DEPTH + 2 * zz + (u - 3)

    def zhop(u, zz, away):
        view, index = block(zz, u)
        return remote(view, view, s_az, arecv.at[index], dp=toward(away))

    def xhop(zz, u, send):
        view, index = block(zz, u)
        return remote(view, view, send, arecv.at[index], dp=across)

    def phop(view, zz):
        return remote(view, view, s_passed, parecv.at[zz], dp=partner)

    def arrived(u, zz):
        xhop(zz, u, s_az).wait_recv()

    def pass_on(u, zz):
        phop(block(zz, u)[0], zz).start()

    def begin(u):
        zhop(u, z, signs[u]).start()
        zhop(u, z, -signs[u]).start()

    def hop(u, distance):
        for side, far in ((signs[u], 4), (-signs[u], 3)):
            if distance > far:
                continue
            zz = at(-side * distance)
            arrived(u, zz)
            if distance < far:
                zhop(u, zz, side).start()
            if u == 2:
                xhop(zz, 2, s_xbottom).start()
            pass_on(u, zz)

    def across_block(zz):
        return nall.at[dp_of(zz, 1 - h, c), BOTTOM], 4 * zz + 2 * (1 - h) + 1

    def from_across(zz):
        view, index = across_block(zz)
        remote(view, view, s_xbottom, arecv.at[index], dp=across).wait_recv()
        phop(view, zz).start()

    def nesterov(part):
        mean = total[0, part, :] * (1.0 / owners)
        following = DECAY * mv[0, part, :] + mean
        new_momentum[0, 0, part, :] = following
        nall[me, part, :] = (mean + DECAY * following).astype(BF16)
    crossed(0)
    total[0, BOTTOM, :] = zlast(2)
    nesterov(BOTTOM)
    begin(2)
    tcopy(0).wait_recv()
    total[0, TOP, :] += trecv[0].astype(F32)
    nesterov(TOP)
    xhop(z, 0, s_xtop).start()
    begin(0)
    xhop(z, 2, s_xbottom).start()

    def strip_of(i):
        return pl.ds(pl.multiple_of(i * strip, strip), strip)

    def scatter(j, i):
        peer = lax.rem(t + i, tensors)
        return remote(
            gpart.at[j, strip_of(peer)], grecv.at[j, t], s_scatter[j], grecv_sem.at[0, j], tensor=peer
        )

    def spread(j, i):
        peer = lax.rem(t + i, tensors)
        return remote(
            gsum.at[j], gall.at[j, strip_of(t)], s_spread[j], grecv_sem.at[1, j], tensor=peer
        )

    def strips(j, phase):
        view = grecv.at[j, pl.ds(0, tensors - 1)]
        return several(view, (s_spread if phase else s_scatter)[j], grecv_sem.at[phase, j])

    def gram(j, value):
        gpart[j] = lax.dot_general(
            value, value, (((1,), (1,)), ((), ())), preferred_element_type=F32
        )
        for i in range(1, tensors):
            scatter(j, i).start()
    gram(0, nall[me])
    pass_on(2, z)
    pass_on(0, z)

    @pl.when(holder)
    def _():
        several(trecv.at[pl.ds(1, 2)], s_top, trecv_sem.at[1]).wait_recv()
        for i, part in ((1, TOP), (2, BOTTOM)):
            value = (total[1, part, :] + trecv[i].astype(F32)) * (GAIN / owners)
            nall[owners + z, part, :] = value.astype(BF16)
        gram(1, nall[owners + z])
        for u in (3, 4):
            xhop(z, u, s_xextra).start()
            begin(u)
            pass_on(u, z)
    arrived(1, z)
    begin(1)
    pass_on(1, z)

    def reduce_strip(j):
        strips(j, 0).wait_recv()
        acc = gpart[j, strip_of(t)]
        for i in range(1, tensors):
            acc = acc + grecv[j, lax.rem(t + i, tensors)]
        gsum[j] = acc
        gall[j, strip_of(t)] = acc
        for i in range(1, tensors):
            spread(j, i).start()
    reduce_strip(0)

    @pl.when(holder)
    def _():
        reduce_strip(1)
    @pl.when(jnp.logical_and(on0, h == 1))
    def _():
        for u in (3, 4):
            arrived(u, z)
            begin(u)
            pass_on(u, z)

    def gather_step(distance, units=(2, 0, 1)):
        for u in units:
            hop(u, distance)

    def gather_extra(distance):
        @pl.when(on0)
        def _():
            for u in (3, 4):
                hop(u, distance)
    gather_step(1, (2, 0))

    def qhop_to(zz, hh, extra, send, dp):
        index = owners + zz if extra else dp_of(zz, hh, c)
        mine = 2 * DEPTH + zz if extra else 2 * zz + hh
        return remote(qall.at[index], qall.at[index], send, qrecv.at[mine], dp=dp)

    def qzhop(zz, away, extra):
        return qhop_to(zz, h, extra, s_qze if extra else s_qz, toward(away))

    def qxhop(zz, hh, extra):
        return qhop_to(zz, hh, extra, s_qxe if extra else s_qx, across)

    def qphop(zz, hh, extra):
        index = owners + zz if extra else dp_of(zz, hh, c)
        return remote(qall.at[index], qall.at[index], s_qpassed, pqrecv.at[zz], dp=partner)

    qsigns = (turn, 1)

    def qbegin(extra):
        sign = qsigns[1 if extra else 0]
        qzhop(z, sign, extra).start()
        qzhop(z, -sign, extra).start()
        qxhop(z, h, extra).start()
        qphop(z, h, extra).start()

    def qhop(distance, extra=False):
        sign = qsigns[1 if extra else 0]
        for side, far in ((sign, 4), (-sign, 3)):
            if distance > far:
                continue
            zz = at(-side * distance)
            qxhop(zz, h, extra).wait_recv()
            if distance < far:
                qzhop(zz, side, extra).start()
            qxhop(zz, h, extra).start()
            qphop(zz, h, extra).start()

    def qacross(zz):
        qxhop(zz, 1 - h, False).wait_recv()
        qphop(zz, 1 - h, False).start()

        @pl.when(jnp.logical_and(on0, h == 1))
        def _():
            qxhop(zz, 0, True).wait_recv()
            qphop(zz, 0, True).start()

    def qstep(distance):
        qhop(distance)

        @pl.when(holder)
        def _():
            qhop(distance, True)

    def finish(js):
        results = polynomials([gall[j] for j in js], factor)
        for j, q in zip(js, results):
            qall[me if j == 0 else owners + z] = q.astype(BF16)
            qbegin(j == 1)
    strips(0, 1).wait_recv()
    @pl.when(holder)
    def _():
        strips(1, 1).wait_recv()
        finish((0, 1))

    @pl.when(jnp.logical_not(holder))
    def _():
        finish((0,))

    def both(distance):
        return (z,) if distance == 0 else (at(4),) if distance == 4 else (at(distance), at(-distance))

    def multiply(index):
        gathered[index] = dot(qall[index], nall[index]).astype(BF16)

    def apply(zz):
        for here, count in ((on0, 2), (on1, 3)):
            @pl.when(here)
            def _():
                several(nall.at[pl.ds(0, count)], s_passed, parecv.at[zz]).wait_recv()
                several(qall.at[pl.ds(0, count)], s_qpassed, pqrecv.at[zz]).wait_recv()

        @pl.loop(0, 2)
        def _(i):
            multiply(4 * zz + 2 * i)
            multiply(4 * zz + 2 * i + 1)

        multiply(owners + zz)

    def crossing(distance):
        for zz in both(distance):
            from_across(zz)

    def qcrossing(distance):
        for zz in both(distance):
            qacross(zz)
    gather_step(1, (1,))
    gather_extra(1)
    gather_step(2)
    gather_extra(2)
    crossing(0)
    crossing(1)
    qstep(1)
    qcrossing(0)
    gather_step(3)
    gather_extra(3)
    qstep(2)
    crossing(2)
    qcrossing(1)
    gather_step(4)
    gather_extra(4)
    qstep(3)
    crossing(3)
    qcrossing(2)
    apply(z)
    qstep(4)
    crossing(4)
    qcrossing(3)
    for zz in both(1):
        apply(zz)
    qcrossing(4)
    for zz in both(2):
        apply(zz)
    for zz in both(3):
        apply(zz)
    apply(at(4))
    has = jnp.float32(0.0)
    which = jnp.int32(0)
    for e in range(DEPTH):
        hit = table[HOLDER, e] == me
        has = jnp.where(hit, 1.0, has)
        which = jnp.where(hit, e, which)
    old = mv[1]
    mean = nall[owners + which].astype(F32) * (1.0 / GAIN) - (DECAY * DECAY / GAIN) * old
    new_momentum[0, 1] = old + has * ((DECAY * old + mean) - old)
    def left(ref, send):
        remote(ref, ref, send, zrecv_sem.at[0, 0], dp=across).wait_send()

    left(xstage, s_x)
    left(xstage, s_xbottom)
    left(xstage.at[0], s_xtop)
    left(qall.at[pl.ds(0, 7)], s_qz)
    left(qall.at[pl.ds(0, DEPTH)], s_qx)
    strips(0, 0).wait_send()
    strips(0, 1).wait_send()

    @pl.when(on1)
    def _():
        left(pstage, s_pair)
        left(zrecv.at[pl.ds(0, 3)], s_z)
        left(zrecv.at[pl.ds(0, 3)], s_az)
        left(tstage.at[0], s_top)
        left(nall.at[pl.ds(0, 16)], s_passed)
        left(qall.at[pl.ds(0, 16)], s_qpassed)

    @pl.when(on0)
    def _():
        left(pstage.at[pl.ds(0, 16)], s_pair)
        left(zrecv, s_z)
        left(zrecv, s_az)
        left(nall.at[pl.ds(0, 24)], s_passed)
        left(qall.at[pl.ds(0, 24)], s_qpassed)

        @pl.when(h == 1)
        def _():
            left(tstage, s_top)

        @pl.when(h == 0)
        def _():
            left(tstage.at[0], s_top)

    @pl.when(holder)
    def _():
        strips(1, 0).wait_send()
        strips(1, 1).wait_send()
        left(xstage.at[pl.ds(0, 2)], s_xextra)
        left(qall.at[pl.ds(0, 7)], s_qze)
        left(qall.at[pl.ds(0, DEPTH)], s_qxe)
def per_device(grads, owner, momentum):
    tensors = lax.axis_size("tensor")
    matrices, rows, cols = grads.shape[1:]
    slots = momentum.shape[1]
    half = rows // 2
    dma = pltpu.SemaphoreType.DMA
    whole = pl.BlockSpec(memory_space=pltpu.VMEM)
    far = pl.BlockSpec(memory_space=pltpu.HBM)
    gathered, new_momentum, table = pl.pallas_call(
        step_kernel,
        out_shape=(
            jax.ShapeDtypeStruct((matrices, rows, cols), BF16),
            jax.ShapeDtypeStruct(momentum.shape, F32),
            jax.ShapeDtypeStruct((8, 128), jnp.int32),
        ),
        in_specs=[whole, far, far],
        out_specs=(whole, whole, whole),
        scratch_shapes=[
            pltpu.VMEM((matrices, rows, cols), BF16),
            pltpu.VMEM((slots, rows, cols), F32),
            pltpu.VMEM((24, rows, cols), BF16),
            pltpu.VMEM((24, rows, cols), BF16),
            pltpu.VMEM((DEPTH, half, cols), BF16),
            pltpu.VMEM((DEPTH, half, cols), BF16),
            pltpu.VMEM((5, 2, half, cols), BF16),
            pltpu.VMEM((5, 7, half, cols), BF16),
            pltpu.VMEM((3, half, cols), BF16),
            pltpu.VMEM((3, half, cols), BF16),
            pltpu.VMEM((2, rows, cols), F32),
            pltpu.VMEM((matrices, rows, cols), BF16),
            pltpu.VMEM((matrices, rows, rows), BF16),
            pltpu.VMEM((2, rows, rows), F32),
            pltpu.VMEM((2, tensors, rows // tensors, rows), F32),
            pltpu.VMEM((2, rows // tensors, rows), F32),
            pltpu.VMEM((2, rows, rows), F32),
            pltpu.SMEM((8, 128), jnp.int32),
            pltpu.VMEM((rows, cols), BF16),
            dma((3,)), dma((18,)), dma((DEPTH,)), dma((DEPTH,)), dma((5, 7)), dma((2,)), dma((2, 2)),
            dma((6 * DEPTH,)), dma((DEPTH,)), dma((3 * DEPTH,)), dma((DEPTH,)),
        ],
        compiler_params=pltpu.CompilerParams(
            collective_id=0, has_side_effects=True, vmem_limit_bytes=46 * 2**20
        ),
        name="step",
    )(owner.reshape(1, matrices), grads, momentum)
    return pl.pallas_call(
        order_kernel,
        out_shape=(
            jax.ShapeDtypeStruct((matrices, rows, cols), BF16),
            jax.ShapeDtypeStruct(momentum.shape, F32),
        ),
        in_specs=[
            pl.BlockSpec(memory_space=pltpu.SMEM),
            pl.BlockSpec(memory_space=pl.ANY),
            pl.BlockSpec(memory_space=pl.ANY),
        ],
        out_specs=(far, far),
        scratch_shapes=[dma((matrices + 1,))],
        compiler_params=pltpu.CompilerParams(vmem_limit_bytes=2**20),
        name="order",
    )(table, gathered, new_momentum)


def solution(mesh):
    in_specs = (P("dp", None, None, "tensor"), P(), P("dp", None, None, "tensor"))
    out_specs = (P(None, None, "tensor"), P("dp", None, None, "tensor"))
    return jax.shard_map(
        per_device, mesh=mesh, in_specs=in_specs, out_specs=out_specs, check_vma=False
    )
```

```python
import functools
import math

import jax
import jax.numpy as jnp
from jax import lax
from jax.experimental import pallas as pl
from jax.experimental.pallas import tpu as pltpu
from jax.sharding import PartitionSpec as P

D = 4096
ITERS = 5
COEF_A = 3.4445
COEF_B = -4.775
COEF_C = 2.0315
EPSILON = 1e-07
DECAY = 0.95

DEPTH = 8
F32 = jnp.float32
BF16 = jnp.bfloat16

GAIN = 1.0 + DECAY

FIRST, SECOND, HOLDER, PLACE = range(4)


def tables(owner, owners, out):
    count = owner.shape[1]

    def grid(shape, dim):
        return lax.broadcasted_iota(jnp.int32, shape, dim)

    def column(row):
        size = row.shape[1]
        square = (size, size)
        kept = jnp.where(grid(square, 0) == grid(square, 1), jnp.broadcast_to(row, square), 0)
        return jnp.sum(kept, axis=1, keepdims=True)

    held = column(owner) == grid((count, owners), 1)
    which = grid((count, owners), 0)
    first = jnp.min(jnp.where(held, which, count - 1), axis=0, keepdims=True)
    last = jnp.max(jnp.where(held, which, -1), axis=0, keepdims=True)
    first_c, last_c = column(first), column(last)
    two = jnp.where(last > first, 1, 0)
    two_c = column(two)
    square = (owners, owners)
    rank = jnp.sum(
        jnp.where(grid(square, 0) < grid(square, 1), jnp.broadcast_to(two_c, square), 0),
        axis=0, keepdims=True,
    )
    rank_c = column(rank)
    eighth = (owners, DEPTH)
    chosen = jnp.logical_and(
        jnp.broadcast_to(rank_c, eighth) == grid(eighth, 1), jnp.broadcast_to(two_c, eighth) > 0
    )
    second = jnp.sum(jnp.where(chosen, jnp.broadcast_to(last_c, eighth), 0), axis=0, keepdims=True)
    holder = jnp.sum(jnp.where(chosen, grid(eighth, 0), 0), axis=0, keepdims=True)
    wide = (owners, count)
    spot = jnp.where(
        jnp.broadcast_to(first_c, wide) == grid(wide, 1), grid(wide, 0), owners + rank_c
    )
    place = jnp.sum(
        jnp.where(jnp.broadcast_to(owner, wide) == grid(wide, 0), spot, 0), axis=0, keepdims=True
    )
    out[FIRST, 0:owners] = first[0]
    out[SECOND, 0:DEPTH] = second[0]
    out[HOLDER, 0:DEPTH] = holder[0]
    out[PLACE, 0:count] = place[0]


def order_kernel(table, in_ref, momentum, out_ref, out_momentum, sems):
    count = out_ref.shape[0]

    def copy(m):
        return pltpu.make_async_copy(in_ref.at[table[PLACE, m]], out_ref.at[m], sems.at[m])

    rest = pltpu.make_async_copy(momentum, out_momentum, sems.at[count])
    for m in range(count):
        copy(m).start()
    rest.start()
    for m in range(count):
        copy(m).wait()
    rest.wait()


def split(a):
    high = a.astype(BF16)
    return high, (a - high.astype(F32)).astype(BF16)


def dot(a, b):
    return jnp.dot(a, b, preferred_element_type=F32)


def product(a, b):
    return dot(a[0], b[0]) + (dot(a[0], b[1]) + dot(a[1], b[0]))


def polynomials(grams, factor):
    size = grams[0].shape[0]
    row = lax.broadcasted_iota(jnp.int32, (size, size), 0)
    col = lax.broadcasted_iota(jnp.int32, (size, size), 1)
    diagonal = row == col
    eye = jnp.where(diagonal, 1.0, 0.0).astype(F32)
    scales, now = [], []
    for gram in grams:
        total = jnp.sum(jnp.where(diagonal, gram, 0.0), keepdims=True)
        scale = 1.0 / (jnp.sqrt(total) + EPSILON)
        scales.append(scale)
        now.append((gram * scale) * scale)
    totals = [None] * len(grams)
    for step in range(ITERS):
        parts = [split(g) for g in now]
        squares = [product(g, g) for g in parts]
        polys = [COEF_A * eye + COEF_B * g + COEF_C * s for g, s in zip(now, squares)]
        poly_parts = [split(p) for p in polys]
        if step + 1 < ITERS:
            once = [product(p, g) for p, g in zip(poly_parts, parts)]
        if step == 0:
            totals = polys
        else:
            totals = [product(p, split(q)) for p, q in zip(poly_parts, totals)]
        if step + 1 < ITERS:
            now = [product(p, split(o)) for p, o in zip(poly_parts, once)]
    return [q * (scale * factor) for q, scale in zip(totals, scales)]


def step_kernel(
    owner_in, grads, momentum, gathered, new_momentum, table_out,
    gv, mv, pstage, precv, xstage, xrecv, zstage, zrecv, tstage, trecv, total,
    nall, qall, gpart, grecv, gsum, gall, table, folded, owner,
    load_sem, sent, precv_sem, xrecv_sem, zrecv_sem, trecv_sem, grecv_sem,
    arecv, parecv, qrecv, pqrecv,
):
    (s_pair, s_x, s_z, s_top, s_az, s_xtop, s_xbottom, s_xextra, s_passed, s_qz, s_qze, s_qx, s_qxe,
     s_qpassed) = (sent.at[i] for i in range(14))
    s_scatter, s_spread = (sent.at[14], sent.at[16]), (sent.at[15], sent.at[17])
    me = lax.axis_index("dp")
    t = lax.axis_index("tensor")
    tensors = lax.axis_size("tensor")
    owners = lax.axis_size("dp")
    c = lax.rem(me, 2)
    h = lax.rem(me // 2, 2)
    z = me // 4
    rows, cols = gv.shape[1], gv.shape[2]
    half = rows // 2
    strip = rows // tensors
    TOP, BOTTOM = pl.ds(0, half), pl.ds(half, half)
    factor = 0.2 * math.sqrt(max(rows, D))
    turn = 1 - 2 * c

    def at(k):
        return lax.rem(z + k + 2 * DEPTH, DEPTH)

    def dp_of(zz, hh, cc):
        return 4 * zz + 2 * hh + cc

    def remote(src, dst, send, recv, dp=None, tensor=None):
        return pltpu.make_async_remote_copy(
            src_ref=src, dst_ref=dst, send_sem=send, recv_sem=recv,
            device_id={"dp": me if dp is None else dp, "tensor": t if tensor is None else tensor},
            device_id_type=pl.DeviceIdType.MESH,
        )

    partner = dp_of(z, h, 1 - c)
    across = dp_of(z, 1 - h, c)
    on0, on1 = c == 0, c == 1
    holder = jnp.logical_and(c == 0, h == 0)

    def toward(k):
        return dp_of(at(k), h, c)
    matrices = gv.shape[0]
    owner_load = pltpu.make_async_copy(owner_in, owner, load_sem.at[3])
    owner_load.start()
    loads = 8
    span = matrices // loads
    for i in range(loads):
        pltpu.make_async_copy(
            grads.at[0, pl.ds(i * span, span)], gv.at[pl.ds(i * span, span)], load_sem.at[0]
        ).start()
    momentum_load = pltpu.make_async_copy(momentum.at[0], mv, load_sem.at[1])
    momentum_load.start()

    barrier = pltpu.get_barrier_semaphore()
    for peer in (partner, across, toward(1), toward(-1)):
        pl.semaphore_signal(
            barrier, inc=1, device_id={"dp": peer, "tensor": t}, device_id_type=pl.DeviceIdType.MESH
        )
    for i in range(1, tensors):
        pl.semaphore_signal(
            barrier, inc=1, device_id={"dp": me, "tensor": lax.rem(t + i, tensors)},
            device_id_type=pl.DeviceIdType.MESH,
        )

    owner_load.wait()
    table_out[...] = jnp.zeros_like(table_out)
    tables(owner[...], owners, table_out)
    to_scalars = pltpu.make_async_copy(table_out, table, load_sem.at[2])
    to_scalars.start()
    pl.semaphore_wait(barrier, 4 + tensors - 1)
    momentum_load.wait()
    folded[...] = (mv[1] * (DECAY * DECAY * owners / GAIN)).astype(BF16)
    to_scalars.wait()
    pltpu.make_async_copy(grads.at[0], gv, load_sem.at[0]).wait()

    order = (4, 3, -3, 2, -2, 1, -1, 0)

    def chosen(row, i):
        return jnp.clip(table[row, i], 0, matrices - 1)

    def extra(zz, part):
        mine = jnp.where(table[HOLDER, zz] == me, 1.0, 0.0).astype(BF16)
        return gv[chosen(SECOND, zz), part, :] + mine * folded[part, :]

    def pair(slot, zz):
        return remote(pstage.at[slot], precv.at[slot], s_pair, precv_sem.at[zz], dp=partner)
    for k in order:
        zz = at(k)
        for hh in range(2):
            pstage[2 * zz + hh] = gv[chosen(FIRST, dp_of(zz, hh, 1 - c))]
            pair(2 * zz + hh, zz).start()

        @pl.when(on1)
        def _():
            for part in (TOP, BOTTOM):
                pstage[16 + zz, part, :] = extra(zz, part)
            pair(16 + zz, zz).start()

    def several(ref, send, recv, dp=partner):
        return remote(ref, ref, send, recv, dp=dp)

    def paired(*offsets):
        for k in offsets:
            for here, matrices in ((on0, 3), (on1, 2)):
                @pl.when(here)
                def _():
                    several(precv.at[pl.ds(0, matrices)], s_pair, precv_sem.at[at(k)]).wait_recv()

    def own(zz, hh, part):
        return gv[chosen(FIRST, dp_of(zz, hh, c)), part, :] + precv[2 * zz + hh, part, :]

    def contribution(u, zz):
        if u == 0:
            return own(zz, h, TOP)
        if u == 1:
            return own(zz, 1 - h, TOP)
        if u == 2:
            return own(zz, h, BOTTOM) + xrecv[zz]
        part = TOP if u == 3 else BOTTOM
        return extra(zz, part) + precv[16 + zz, part, :]

    signs = (1, -1, turn, 1, -1)

    def zcopy(u, slot, src, k):
        return remote(src, zrecv.at[u, slot], s_z, zrecv_sem.at[u, slot], dp=toward(k))

    def zwait(u, slot):
        zcopy(u, slot, zrecv.at[u, slot], signs[u]).wait_recv()

    def first(u, place, slot, k, away):
        zstage[u, place] = contribution(u, at(k))
        zcopy(u, slot, zstage.at[u, place], away).start()

    def passed(u, slot, k, away):
        zwait(u, slot)
        zrecv[u, slot] = zrecv[u, slot] + contribution(u, at(k))
        zcopy(u, slot + 1, zrecv.at[u, slot], away).start()

    def z4(u):
        first(u, 0, 0, 4 * signs[u], signs[u])

    def z3b(u):
        first(u, 1, 4, -3 * signs[u], -signs[u])

    def z3a(u):
        passed(u, 0, 3 * signs[u], signs[u])

    def z3(u):
        z3b(u)
        z3a(u)

    def z2(u):
        passed(u, 1, 2 * signs[u], signs[u])
        passed(u, 4, -2 * signs[u], -signs[u])

    def z1(u):
        passed(u, 2, signs[u], signs[u])
        passed(u, 5, -signs[u], -signs[u])

    def zlast(u):
        zwait(u, 3)
        zwait(u, 6)
        return contribution(u, z).astype(F32) + (zrecv[u, 3].astype(F32) + zrecv[u, 6].astype(F32))

    def xcopy(zz):
        return remote(xstage.at[zz], xrecv.at[zz], s_x, xrecv_sem.at[zz], dp=across)

    def xstep(*offsets):
        for k in offsets:
            zz = at(k)
            xstage[zz] = own(zz, 1 - h, BOTTOM)
            xcopy(zz).start()

    def crossed(*offsets):
        for k in offsets:
            xcopy(at(k)).wait_recv()

    def every(step):
        step(0)
        step(1)

        @pl.when(on0)
        def _():
            step(3)
            step(4)
    paired(4)
    every(z4)
    xstep(4)
    paired(3, -3)
    every(z3b)
    xstep(3, -3)
    every(z3a)
    paired(2, -2)
    xstep(2, -2)
    paired(1, -1)
    xstep(1, -1)
    crossed(4)
    z4(2)
    every(z2)
    paired(0)
    xstep(0)
    crossed(3, -3)
    z3(2)
    z1(1)

    @pl.when(on0)
    def _():
        z1(3)
        z1(4)
    crossed(2, -2)
    z2(2)
    z1(0)
    crossed(1, -1)
    z1(2)

    def tcopy(i):
        return remote(
            tstage.at[i], trecv.at[i], s_top, trecv_sem.at[0 if i == 0 else 1], dp=across
        )
    tstage[0] = zlast(1).astype(BF16)
    tcopy(0).start()

    @pl.when(on0)
    def _():
        for i, part in ((1, TOP), (2, BOTTOM)):
            partial = zlast(2 + i)

            @pl.when(h == 1)
            def _():
                tstage[i] = partial.astype(BF16)
                tcopy(i).start()

            @pl.when(h == 0)
            def _():
                total[1, part, :] = partial

    total[0, TOP, :] = zlast(0)

    def block(zz, u):
        if u < 3:
            hh = 1 - h if u == 1 else h
            lower = 1 if u == 2 else 0
            return nall.at[dp_of(zz, hh, c), BOTTOM if lower else TOP], 4 * zz + 2 * hh + lower
        return nall.at[owners + zz, TOP if u == 3 else BOTTOM], 4 * DEPTH + 2 * zz + (u - 3)

    def zhop(u, zz, away):
        view, index = block(zz, u)
        return remote(view, view, s_az, arecv.at[index], dp=toward(away))

    def xhop(zz, u, send):
        view, index = block(zz, u)
        return remote(view, view, send, arecv.at[index], dp=across)

    def phop(view, zz):
        return remote(view, view, s_passed, parecv.at[zz], dp=partner)

    def arrived(u, zz):
        xhop(zz, u, s_az).wait_recv()

    def pass_on(u, zz):
        phop(block(zz, u)[0], zz).start()

    def begin(u):
        zhop(u, z, signs[u]).start()
        zhop(u, z, -signs[u]).start()

    def hop(u, distance):
        for side, far in ((signs[u], 4), (-signs[u], 3)):
            if distance > far:
                continue
            zz = at(-side * distance)
            arrived(u, zz)
            if distance < far:
                zhop(u, zz, side).start()
            if u == 2:
                xhop(zz, 2, s_xbottom).start()
            pass_on(u, zz)

    def across_block(zz):
        return nall.at[dp_of(zz, 1 - h, c), BOTTOM], 4 * zz + 2 * (1 - h) + 1

    def from_across(zz):
        view, index = across_block(zz)
        remote(view, view, s_xbottom, arecv.at[index], dp=across).wait_recv()
        phop(view, zz).start()

    def nesterov(part):
        mean = total[0, part, :] * (1.0 / owners)
        following = DECAY * mv[0, part, :] + mean
        new_momentum[0, 0, part, :] = following
        nall[me, part, :] = (mean + DECAY * following).astype(BF16)
    crossed(0)
    total[0, BOTTOM, :] = zlast(2)
    nesterov(BOTTOM)
    begin(2)
    tcopy(0).wait_recv()
    total[0, TOP, :] += trecv[0].astype(F32)
    nesterov(TOP)
    xhop(z, 0, s_xtop).start()
    begin(0)
    xhop(z, 2, s_xbottom).start()

    def strip_of(i):
        return pl.ds(pl.multiple_of(i * strip, strip), strip)

    def scatter(j, i):
        peer = lax.rem(t + i, tensors)
        return remote(
            gpart.at[j, strip_of(peer)], grecv.at[j, t], s_scatter[j], grecv_sem.at[0, j], tensor=peer
        )

    def spread(j, i):
        peer = lax.rem(t + i, tensors)
        return remote(
            gsum.at[j], gall.at[j, strip_of(t)], s_spread[j], grecv_sem.at[1, j], tensor=peer
        )

    def strips(j, phase):
        view = grecv.at[j, pl.ds(0, tensors - 1)]
        return several(view, (s_spread if phase else s_scatter)[j], grecv_sem.at[phase, j])

    def gram(j, value):
        gpart[j] = lax.dot_general(
            value, value, (((1,), (1,)), ((), ())), preferred_element_type=F32
        )
        for i in range(1, tensors):
            scatter(j, i).start()
    gram(0, nall[me])
    pass_on(2, z)
    pass_on(0, z)

    @pl.when(holder)
    def _():
        several(trecv.at[pl.ds(1, 2)], s_top, trecv_sem.at[1]).wait_recv()
        for i, part in ((1, TOP), (2, BOTTOM)):
            value = (total[1, part, :] + trecv[i].astype(F32)) * (GAIN / owners)
            nall[owners + z, part, :] = value.astype(BF16)
        gram(1, nall[owners + z])
        for u in (3, 4):
            xhop(z, u, s_xextra).start()
            begin(u)
            pass_on(u, z)
    arrived(1, z)
    begin(1)
    pass_on(1, z)

    def reduce_strip(j):
        strips(j, 0).wait_recv()
        acc = gpart[j, strip_of(t)]
        for i in range(1, tensors):
            acc = acc + grecv[j, lax.rem(t + i, tensors)]
        gsum[j] = acc
        gall[j, strip_of(t)] = acc
        for i in range(1, tensors):
            spread(j, i).start()
    reduce_strip(0)

    @pl.when(holder)
    def _():
        reduce_strip(1)
    @pl.when(jnp.logical_and(on0, h == 1))
    def _():
        for u in (3, 4):
            arrived(u, z)
            begin(u)
            pass_on(u, z)

    def gather_step(distance, units=(2, 0, 1)):
        for u in units:
            hop(u, distance)

    def gather_extra(distance):
        @pl.when(on0)
        def _():
            for u in (3, 4):
                hop(u, distance)
    gather_step(1, (2, 0))

    def qhop_to(zz, hh, extra, send, dp):
        index = owners + zz if extra else dp_of(zz, hh, c)
        mine = 2 * DEPTH + zz if extra else 2 * zz + hh
        return remote(qall.at[index], qall.at[index], send, qrecv.at[mine], dp=dp)

    def qzhop(zz, away, extra):
        return qhop_to(zz, h, extra, s_qze if extra else s_qz, toward(away))

    def qxhop(zz, hh, extra):
        return qhop_to(zz, hh, extra, s_qxe if extra else s_qx, across)

    def qphop(zz, hh, extra):
        index = owners + zz if extra else dp_of(zz, hh, c)
        return remote(qall.at[index], qall.at[index], s_qpassed, pqrecv.at[zz], dp=partner)

    qsigns = (turn, 1)

    def qbegin(extra):
        sign = qsigns[1 if extra else 0]
        qzhop(z, sign, extra).start()
        qzhop(z, -sign, extra).start()
        qxhop(z, h, extra).start()
        qphop(z, h, extra).start()

    def qhop(distance, extra=False):
        sign = qsigns[1 if extra else 0]
        for side, far in ((sign, 4), (-sign, 3)):
            if distance > far:
                continue
            zz = at(-side * distance)
            qxhop(zz, h, extra).wait_recv()
            if distance < far:
                qzhop(zz, side, extra).start()
            qxhop(zz, h, extra).start()
            qphop(zz, h, extra).start()

    def qacross(zz):
        qxhop(zz, 1 - h, False).wait_recv()
        qphop(zz, 1 - h, False).start()

        @pl.when(jnp.logical_and(on0, h == 1))
        def _():
            qxhop(zz, 0, True).wait_recv()
            qphop(zz, 0, True).start()

    def qstep(distance):
        qhop(distance)

        @pl.when(holder)
        def _():
            qhop(distance, True)

    def finish(js):
        results = polynomials([gall[j] for j in js], factor)
        for j, q in zip(js, results):
            qall[me if j == 0 else owners + z] = q.astype(BF16)
            qbegin(j == 1)
    strips(0, 1).wait_recv()
    @pl.when(holder)
    def _():
        strips(1, 1).wait_recv()
        finish((0, 1))

    @pl.when(jnp.logical_not(holder))
    def _():
        finish((0,))

    def both(distance):
        return (z,) if distance == 0 else (at(4),) if distance == 4 else (at(distance), at(-distance))

    def multiply(index):
        gathered[index] = dot(qall[index], nall[index]).astype(BF16)

    def apply(zz):
        for here, count in ((on0, 2), (on1, 3)):
            @pl.when(here)
            def _():
                several(nall.at[pl.ds(0, count)], s_passed, parecv.at[zz]).wait_recv()
                several(qall.at[pl.ds(0, count)], s_qpassed, pqrecv.at[zz]).wait_recv()

        @pl.loop(0, 2)
        def _(i):
            multiply(4 * zz + 2 * i)
            multiply(4 * zz + 2 * i + 1)

        multiply(owners + zz)

    def crossing(distance):
        for zz in both(distance):
            from_across(zz)

    def qcrossing(distance):
        for zz in both(distance):
            qacross(zz)
    gather_step(1, (1,))
    gather_extra(1)
    hop(2, 2)
    crossing(0)
    crossing(1)
    qstep(1)
    gather_step(2, (0, 1))
    qcrossing(0)
    gather_extra(2)
    qstep(2)
    qcrossing(1)
    hop(2, 3)
    hop(0, 3)
    crossing(2)
    qstep(3)
    hop(1, 3)
    gather_extra(3)
    apply(z)
    hop(2, 4)
    crossing(3)
    qcrossing(2)
    qstep(4)
    gather_step(4, (0, 1))
    gather_extra(4)
    for zz in both(1):
        apply(zz)
    crossing(4)
    qcrossing(3)
    for zz in both(2):
        apply(zz)
    qcrossing(4)
    for zz in both(3):
        apply(zz)
    apply(at(4))
    has = jnp.float32(0.0)
    which = jnp.int32(0)
    for e in range(DEPTH):
        hit = table[HOLDER, e] == me
        has = jnp.where(hit, 1.0, has)
        which = jnp.where(hit, e, which)
    old = mv[1]
    mean = nall[owners + which].astype(F32) * (1.0 / GAIN) - (DECAY * DECAY / GAIN) * old
    new_momentum[0, 1] = old + has * ((DECAY * old + mean) - old)
    def left(ref, send):
        remote(ref, ref, send, zrecv_sem.at[0, 0], dp=across).wait_send()

    left(xstage, s_x)
    left(xstage, s_xbottom)
    left(xstage.at[0], s_xtop)
    left(qall.at[pl.ds(0, 7)], s_qz)
    left(qall.at[pl.ds(0, DEPTH)], s_qx)
    strips(0, 0).wait_send()
    strips(0, 1).wait_send()

    @pl.when(on1)
    def _():
        left(pstage, s_pair)
        left(zrecv.at[pl.ds(0, 3)], s_z)
        left(zrecv.at[pl.ds(0, 3)], s_az)
        left(tstage.at[0], s_top)
        left(nall.at[pl.ds(0, 16)], s_passed)
        left(qall.at[pl.ds(0, 16)], s_qpassed)

    @pl.when(on0)
    def _():
        left(pstage.at[pl.ds(0, 16)], s_pair)
        left(zrecv, s_z)
        left(zrecv, s_az)
        left(nall.at[pl.ds(0, 24)], s_passed)
        left(qall.at[pl.ds(0, 24)], s_qpassed)

        @pl.when(h == 1)
        def _():
            left(tstage, s_top)

        @pl.when(h == 0)
        def _():
            left(tstage.at[0], s_top)

    @pl.when(holder)
    def _():
        strips(1, 0).wait_send()
        strips(1, 1).wait_send()
        left(xstage.at[pl.ds(0, 2)], s_xextra)
        left(qall.at[pl.ds(0, 7)], s_qze)
        left(qall.at[pl.ds(0, DEPTH)], s_qxe)
def per_device(grads, owner, momentum):
    tensors = lax.axis_size("tensor")
    matrices, rows, cols = grads.shape[1:]
    slots = momentum.shape[1]
    half = rows // 2
    dma = pltpu.SemaphoreType.DMA
    whole = pl.BlockSpec(memory_space=pltpu.VMEM)
    far = pl.BlockSpec(memory_space=pltpu.HBM)
    gathered, new_momentum, table = pl.pallas_call(
        step_kernel,
        out_shape=(
            jax.ShapeDtypeStruct((matrices, rows, cols), BF16),
            jax.ShapeDtypeStruct(momentum.shape, F32),
            jax.ShapeDtypeStruct((8, 128), jnp.int32),
        ),
        in_specs=[far, far, far],
        out_specs=(whole, whole, whole),
        scratch_shapes=[
            pltpu.VMEM((matrices, rows, cols), BF16),
            pltpu.VMEM((slots, rows, cols), F32),
            pltpu.VMEM((24, rows, cols), BF16),
            pltpu.VMEM((24, rows, cols), BF16),
            pltpu.VMEM((DEPTH, half, cols), BF16),
            pltpu.VMEM((DEPTH, half, cols), BF16),
            pltpu.VMEM((5, 2, half, cols), BF16),
            pltpu.VMEM((5, 7, half, cols), BF16),
            pltpu.VMEM((3, half, cols), BF16),
            pltpu.VMEM((3, half, cols), BF16),
            pltpu.VMEM((2, rows, cols), F32),
            pltpu.VMEM((matrices, rows, cols), BF16),
            pltpu.VMEM((matrices, rows, rows), BF16),
            pltpu.VMEM((2, rows, rows), F32),
            pltpu.VMEM((2, tensors, rows // tensors, rows), F32),
            pltpu.VMEM((2, rows // tensors, rows), F32),
            pltpu.VMEM((2, rows, rows), F32),
            pltpu.SMEM((8, 128), jnp.int32),
            pltpu.VMEM((rows, cols), BF16),
            pltpu.VMEM((1, matrices), jnp.int32),
            dma((4,)), dma((18,)), dma((DEPTH,)), dma((DEPTH,)), dma((5, 7)), dma((2,)), dma((2, 2)),
            dma((6 * DEPTH,)), dma((DEPTH,)), dma((3 * DEPTH,)), dma((DEPTH,)),
        ],
        compiler_params=pltpu.CompilerParams(
            collective_id=0, has_side_effects=True, vmem_limit_bytes=46 * 2**20
        ),
        name="step",
    )(*(pltpu.with_memory_space_constraint(a, pltpu.HBM) for a in (owner.reshape(1, matrices), grads, momentum)))
    return pl.pallas_call(
        order_kernel,
        out_shape=(
            jax.ShapeDtypeStruct((matrices, rows, cols), BF16),
            jax.ShapeDtypeStruct(momentum.shape, F32),
        ),
        in_specs=[
            pl.BlockSpec(memory_space=pltpu.SMEM),
            pl.BlockSpec(memory_space=pl.ANY),
            pl.BlockSpec(memory_space=pl.ANY),
        ],
        out_specs=(far, far),
        scratch_shapes=[dma((matrices + 1,))],
        compiler_params=pltpu.CompilerParams(vmem_limit_bytes=2**20),
        name="order",
    )(table, gathered, new_momentum)


def solution(mesh):
    in_specs = (P("dp", None, None, "tensor"), P(), P("dp", None, None, "tensor"))
    out_specs = (P(None, None, "tensor"), P("dp", None, None, "tensor"))
    return jax.shard_map(
        per_device, mesh=mesh, in_specs=in_specs, out_specs=out_specs, check_vma=False
    )
```

```python
import functools
import math

import jax
import jax.numpy as jnp
from jax import lax
from jax.experimental import pallas as pl
from jax.experimental.pallas import tpu as pltpu
from jax.sharding import PartitionSpec as P

D = 4096
ITERS = 5
COEF_A = 3.4445
COEF_B = -4.775
COEF_C = 2.0315
EPSILON = 1e-07
DECAY = 0.95

DEPTH = 8
F32 = jnp.float32
BF16 = jnp.bfloat16

GAIN = 1.0 + DECAY

FIRST, SECOND, HOLDER, PLACE = range(4)


def tables(owner, owners, out):
    count = owner.shape[1]

    def grid(shape, dim):
        return lax.broadcasted_iota(jnp.int32, shape, dim)

    def column(row):
        size = row.shape[1]
        square = (size, size)
        kept = jnp.where(grid(square, 0) == grid(square, 1), jnp.broadcast_to(row, square), 0)
        return jnp.sum(kept, axis=1, keepdims=True)

    held = column(owner) == grid((count, owners), 1)
    which = grid((count, owners), 0)
    first = jnp.min(jnp.where(held, which, count - 1), axis=0, keepdims=True)
    last = jnp.max(jnp.where(held, which, -1), axis=0, keepdims=True)
    first_c, last_c = column(first), column(last)
    two = jnp.where(last > first, 1, 0)
    two_c = column(two)
    square = (owners, owners)
    rank = jnp.sum(
        jnp.where(grid(square, 0) < grid(square, 1), jnp.broadcast_to(two_c, square), 0),
        axis=0, keepdims=True,
    )
    rank_c = column(rank)
    eighth = (owners, DEPTH)
    chosen = jnp.logical_and(
        jnp.broadcast_to(rank_c, eighth) == grid(eighth, 1), jnp.broadcast_to(two_c, eighth) > 0
    )
    second = jnp.sum(jnp.where(chosen, jnp.broadcast_to(last_c, eighth), 0), axis=0, keepdims=True)
    holder = jnp.sum(jnp.where(chosen, grid(eighth, 0), 0), axis=0, keepdims=True)
    wide = (owners, count)
    spot = jnp.where(
        jnp.broadcast_to(first_c, wide) == grid(wide, 1), grid(wide, 0), owners + rank_c
    )
    place = jnp.sum(
        jnp.where(jnp.broadcast_to(owner, wide) == grid(wide, 0), spot, 0), axis=0, keepdims=True
    )
    out[FIRST, 0:owners] = first[0]
    out[SECOND, 0:DEPTH] = second[0]
    out[HOLDER, 0:DEPTH] = holder[0]
    out[PLACE, 0:count] = place[0]


def order_kernel(table, in_ref, momentum, out_ref, out_momentum, sems):
    count = out_ref.shape[0]

    def copy(m):
        return pltpu.make_async_copy(in_ref.at[table[PLACE, m]], out_ref.at[m], sems.at[m])

    rest = pltpu.make_async_copy(momentum, out_momentum, sems.at[count])
    for m in range(count):
        copy(m).start()
    rest.start()
    for m in range(count):
        copy(m).wait()
    rest.wait()


def split(a):
    high = a.astype(BF16)
    return high, (a - high.astype(F32)).astype(BF16)


def dot(a, b):
    return jnp.dot(a, b, preferred_element_type=F32)


def product(a, b):
    return dot(jnp.concatenate([a[0], a[1], a[0]], axis=1), jnp.concatenate([b[0], b[0], b[1]], axis=0))


def polynomials(grams, factor):
    size = grams[0].shape[0]
    row = lax.broadcasted_iota(jnp.int32, (size, size), 0)
    col = lax.broadcasted_iota(jnp.int32, (size, size), 1)
    diagonal = row == col
    eye = jnp.where(diagonal, 1.0, 0.0).astype(F32)
    scales, now = [], []
    for gram in grams:
        total = jnp.sum(jnp.where(diagonal, gram, 0.0), keepdims=True)
        scale = 1.0 / (jnp.sqrt(total) + EPSILON)
        scales.append(scale)
        now.append((gram * scale) * scale)
    totals = [None] * len(grams)
    for step in range(ITERS):
        parts = [split(g) for g in now]
        squares = [product(g, g) for g in parts]
        polys = [COEF_A * eye + COEF_B * g + COEF_C * s for g, s in zip(now, squares)]
        poly_parts = [split(p) for p in polys]
        if step + 1 < ITERS:
            once = [product(p, g) for p, g in zip(poly_parts, parts)]
        if step == 0:
            totals = polys
        else:
            totals = [product(p, split(q)) for p, q in zip(poly_parts, totals)]
        if step + 1 < ITERS:
            now = [product(p, split(o)) for p, o in zip(poly_parts, once)]
    return [q * (scale * factor) for q, scale in zip(totals, scales)]


def step_kernel(
    owner_in, grads, momentum, gathered, new_momentum, table_out,
    gv, mv, pstage, precv, xstage, xrecv, zstage, zrecv, tstage, trecv, total,
    nall, qall, gpart, grecv, gsum, gall, table, folded, owner,
    load_sem, sent, precv_sem, xrecv_sem, zrecv_sem, trecv_sem, grecv_sem,
    arecv, parecv, qrecv, pqrecv,
):
    (s_pair, s_x, s_z, s_top, s_az, s_xtop, s_xbottom, s_xextra, s_passed, s_qz, s_qze, s_qx, s_qxe,
     s_qpassed) = (sent.at[i] for i in range(14))
    s_scatter, s_spread = (sent.at[14], sent.at[16]), (sent.at[15], sent.at[17])
    me = lax.axis_index("dp")
    t = lax.axis_index("tensor")
    tensors = lax.axis_size("tensor")
    owners = lax.axis_size("dp")
    c = lax.rem(me, 2)
    h = lax.rem(me // 2, 2)
    z = me // 4
    rows, cols = gv.shape[1], gv.shape[2]
    half = rows // 2
    strip = rows // tensors
    TOP, BOTTOM = pl.ds(0, half), pl.ds(half, half)
    factor = 0.2 * math.sqrt(max(rows, D))
    turn = 1 - 2 * c

    def at(k):
        return lax.rem(z + k + 2 * DEPTH, DEPTH)

    def dp_of(zz, hh, cc):
        return 4 * zz + 2 * hh + cc

    def remote(src, dst, send, recv, dp=None, tensor=None):
        return pltpu.make_async_remote_copy(
            src_ref=src, dst_ref=dst, send_sem=send, recv_sem=recv,
            device_id={"dp": me if dp is None else dp, "tensor": t if tensor is None else tensor},
            device_id_type=pl.DeviceIdType.MESH,
        )

    partner = dp_of(z, h, 1 - c)
    across = dp_of(z, 1 - h, c)
    on0, on1 = c == 0, c == 1
    holder = jnp.logical_and(c == 0, h == 0)

    def toward(k):
        return dp_of(at(k), h, c)
    matrices = gv.shape[0]
    owner_load = pltpu.make_async_copy(owner_in, owner, load_sem.at[3])
    owner_load.start()
    loads = 8
    span = matrices // loads
    for i in range(loads):
        pltpu.make_async_copy(
            grads.at[0, pl.ds(i * span, span)], gv.at[pl.ds(i * span, span)], load_sem.at[0]
        ).start()
    momentum_load = pltpu.make_async_copy(momentum.at[0], mv, load_sem.at[1])
    momentum_load.start()

    barrier = pltpu.get_barrier_semaphore()
    for peer in (partner, across, toward(1), toward(-1)):
        pl.semaphore_signal(
            barrier, inc=1, device_id={"dp": peer, "tensor": t}, device_id_type=pl.DeviceIdType.MESH
        )
    for i in range(1, tensors):
        pl.semaphore_signal(
            barrier, inc=1, device_id={"dp": me, "tensor": lax.rem(t + i, tensors)},
            device_id_type=pl.DeviceIdType.MESH,
        )

    owner_load.wait()
    table_out[...] = jnp.zeros_like(table_out)
    tables(owner[...], owners, table_out)
    to_scalars = pltpu.make_async_copy(table_out, table, load_sem.at[2])
    to_scalars.start()
    pl.semaphore_wait(barrier, 4 + tensors - 1)
    momentum_load.wait()
    folded[...] = (mv[1] * (DECAY * DECAY * owners / GAIN)).astype(BF16)
    to_scalars.wait()
    pltpu.make_async_copy(grads.at[0], gv, load_sem.at[0]).wait()

    order = (4, 3, -3, 2, -2, 1, -1, 0)

    def chosen(row, i):
        return jnp.clip(table[row, i], 0, matrices - 1)

    def extra(zz, part):
        mine = jnp.where(table[HOLDER, zz] == me, 1.0, 0.0).astype(BF16)
        return gv[chosen(SECOND, zz), part, :] + mine * folded[part, :]

    def pair(slot, zz):
        return remote(pstage.at[slot], precv.at[slot], s_pair, precv_sem.at[zz], dp=partner)
    for k in order:
        zz = at(k)
        for hh in range(2):
            pstage[2 * zz + hh] = gv[chosen(FIRST, dp_of(zz, hh, 1 - c))]
            pair(2 * zz + hh, zz).start()

        @pl.when(on1)
        def _():
            for part in (TOP, BOTTOM):
                pstage[16 + zz, part, :] = extra(zz, part)
            pair(16 + zz, zz).start()

    def several(ref, send, recv, dp=partner):
        return remote(ref, ref, send, recv, dp=dp)

    def paired(*offsets):
        for k in offsets:
            for here, matrices in ((on0, 3), (on1, 2)):
                @pl.when(here)
                def _():
                    several(precv.at[pl.ds(0, matrices)], s_pair, precv_sem.at[at(k)]).wait_recv()

    def own(zz, hh, part):
        return gv[chosen(FIRST, dp_of(zz, hh, c)), part, :] + precv[2 * zz + hh, part, :]

    def contribution(u, zz):
        if u == 0:
            return own(zz, h, TOP)
        if u == 1:
            return own(zz, 1 - h, TOP)
        if u == 2:
            return own(zz, h, BOTTOM) + xrecv[zz]
        part = TOP if u == 3 else BOTTOM
        return extra(zz, part) + precv[16 + zz, part, :]

    signs = (1, -1, turn, 1, -1)

    def zcopy(u, slot, src, k):
        return remote(src, zrecv.at[u, slot], s_z, zrecv_sem.at[u, slot], dp=toward(k))

    def zwait(u, slot):
        zcopy(u, slot, zrecv.at[u, slot], signs[u]).wait_recv()

    def first(u, place, slot, k, away):
        zstage[u, place] = contribution(u, at(k))
        zcopy(u, slot, zstage.at[u, place], away).start()

    def passed(u, slot, k, away):
        zwait(u, slot)
        zrecv[u, slot] = zrecv[u, slot] + contribution(u, at(k))
        zcopy(u, slot + 1, zrecv.at[u, slot], away).start()

    def z4(u):
        first(u, 0, 0, 4 * signs[u], signs[u])

    def z3b(u):
        first(u, 1, 4, -3 * signs[u], -signs[u])

    def z3a(u):
        passed(u, 0, 3 * signs[u], signs[u])

    def z3(u):
        z3b(u)
        z3a(u)

    def z2(u):
        passed(u, 1, 2 * signs[u], signs[u])
        passed(u, 4, -2 * signs[u], -signs[u])

    def z1(u):
        passed(u, 2, signs[u], signs[u])
        passed(u, 5, -signs[u], -signs[u])

    def zlast(u):
        zwait(u, 3)
        zwait(u, 6)
        return contribution(u, z).astype(F32) + (zrecv[u, 3].astype(F32) + zrecv[u, 6].astype(F32))

    def xcopy(zz):
        return remote(xstage.at[zz], xrecv.at[zz], s_x, xrecv_sem.at[zz], dp=across)

    def xstep(*offsets):
        for k in offsets:
            zz = at(k)
            xstage[zz] = own(zz, 1 - h, BOTTOM)
            xcopy(zz).start()

    def crossed(*offsets):
        for k in offsets:
            xcopy(at(k)).wait_recv()

    def every(step):
        step(0)
        step(1)

        @pl.when(on0)
        def _():
            step(3)
            step(4)
    paired(4)
    every(z4)
    xstep(4)
    paired(3, -3)
    every(z3b)
    xstep(3, -3)
    every(z3a)
    paired(2, -2)
    xstep(2, -2)
    paired(1, -1)
    xstep(1, -1)
    crossed(4)
    z4(2)
    every(z2)
    paired(0)
    xstep(0)
    crossed(3, -3)
    z3(2)
    z1(1)

    @pl.when(on0)
    def _():
        z1(3)
        z1(4)
    crossed(2, -2)
    z2(2)
    z1(0)
    crossed(1, -1)
    z1(2)

    def tcopy(i):
        return remote(
            tstage.at[i], trecv.at[i], s_top, trecv_sem.at[0 if i == 0 else 1], dp=across
        )
    tstage[0] = zlast(1).astype(BF16)
    tcopy(0).start()

    @pl.when(on0)
    def _():
        for i, part in ((1, TOP), (2, BOTTOM)):
            partial = zlast(2 + i)

            @pl.when(h == 1)
            def _():
                tstage[i] = partial.astype(BF16)
                tcopy(i).start()

            @pl.when(h == 0)
            def _():
                total[1, part, :] = partial

    total[0, TOP, :] = zlast(0)

    def block(zz, u):
        if u < 3:
            hh = 1 - h if u == 1 else h
            lower = 1 if u == 2 else 0
            return nall.at[dp_of(zz, hh, c), BOTTOM if lower else TOP], 4 * zz + 2 * hh + lower
        return nall.at[owners + zz, TOP if u == 3 else BOTTOM], 4 * DEPTH + 2 * zz + (u - 3)

    def zhop(u, zz, away):
        view, index = block(zz, u)
        return remote(view, view, s_az, arecv.at[index], dp=toward(away))

    def xhop(zz, u, send):
        view, index = block(zz, u)
        return remote(view, view, send, arecv.at[index], dp=across)

    def phop(view, zz):
        return remote(view, view, s_passed, parecv.at[zz], dp=partner)

    def arrived(u, zz):
        xhop(zz, u, s_az).wait_recv()

    def pass_on(u, zz):
        phop(block(zz, u)[0], zz).start()

    def begin(u):
        zhop(u, z, signs[u]).start()
        zhop(u, z, -signs[u]).start()

    def hop(u, distance):
        for side, far in ((signs[u], 4), (-signs[u], 3)):
            if distance > far:
                continue
            zz = at(-side * distance)
            arrived(u, zz)
            if distance < far:
                zhop(u, zz, side).start()
            if u == 2:
                xhop(zz, 2, s_xbottom).start()
            pass_on(u, zz)

    def across_block(zz):
        return nall.at[dp_of(zz, 1 - h, c), BOTTOM], 4 * zz + 2 * (1 - h) + 1

    def from_across(zz):
        view, index = across_block(zz)
        remote(view, view, s_xbottom, arecv.at[index], dp=across).wait_recv()
        phop(view, zz).start()

    def nesterov(part):
        mean = total[0, part, :] * (1.0 / owners)
        following = DECAY * mv[0, part, :] + mean
        new_momentum[0, 0, part, :] = following
        nall[me, part, :] = (mean + DECAY * following).astype(BF16)
    crossed(0)
    total[0, BOTTOM, :] = zlast(2)
    nesterov(BOTTOM)
    begin(2)
    tcopy(0).wait_recv()
    total[0, TOP, :] += trecv[0].astype(F32)
    nesterov(TOP)
    xhop(z, 0, s_xtop).start()
    begin(0)
    xhop(z, 2, s_xbottom).start()

    def strip_of(i):
        return pl.ds(pl.multiple_of(i * strip, strip), strip)

    def scatter(j, i):
        peer = lax.rem(t + i, tensors)
        return remote(
            gpart.at[j, strip_of(peer)], grecv.at[j, t], s_scatter[j], grecv_sem.at[0, j], tensor=peer
        )

    def spread(j, i):
        peer = lax.rem(t + i, tensors)
        return remote(
            gsum.at[j], gall.at[j, strip_of(t)], s_spread[j], grecv_sem.at[1, j], tensor=peer
        )

    def strips(j, phase):
        view = grecv.at[j, pl.ds(0, tensors - 1)]
        return several(view, (s_spread if phase else s_scatter)[j], grecv_sem.at[phase, j])

    def gram(j, value):
        gpart[j] = lax.dot_general(
            value, value, (((1,), (1,)), ((), ())), preferred_element_type=F32
        )
        for i in range(1, tensors):
            scatter(j, i).start()
    gram(0, nall[me])
    pass_on(2, z)
    pass_on(0, z)

    @pl.when(holder)
    def _():
        several(trecv.at[pl.ds(1, 2)], s_top, trecv_sem.at[1]).wait_recv()
        for i, part in ((1, TOP), (2, BOTTOM)):
            value = (total[1, part, :] + trecv[i].astype(F32)) * (GAIN / owners)
            nall[owners + z, part, :] = value.astype(BF16)
        gram(1, nall[owners + z])
        for u in (3, 4):
            xhop(z, u, s_xextra).start()
            begin(u)
            pass_on(u, z)
    arrived(1, z)
    begin(1)
    pass_on(1, z)

    def reduce_strip(j):
        strips(j, 0).wait_recv()
        acc = gpart[j, strip_of(t)]
        for i in range(1, tensors):
            acc = acc + grecv[j, lax.rem(t + i, tensors)]
        gsum[j] = acc
        gall[j, strip_of(t)] = acc
        for i in range(1, tensors):
            spread(j, i).start()
    reduce_strip(0)

    @pl.when(holder)
    def _():
        reduce_strip(1)
    @pl.when(jnp.logical_and(on0, h == 1))
    def _():
        for u in (3, 4):
            arrived(u, z)
            begin(u)
            pass_on(u, z)

    def gather_step(distance, units=(2, 0, 1)):
        for u in units:
            hop(u, distance)

    def gather_extra(distance):
        @pl.when(on0)
        def _():
            for u in (3, 4):
                hop(u, distance)
    gather_step(1, (2, 0))

    def qhop_to(zz, hh, extra, send, dp):
        index = owners + zz if extra else dp_of(zz, hh, c)
        mine = 2 * DEPTH + zz if extra else 2 * zz + hh
        return remote(qall.at[index], qall.at[index], send, qrecv.at[mine], dp=dp)

    def qzhop(zz, away, extra):
        return qhop_to(zz, h, extra, s_qze if extra else s_qz, toward(away))

    def qxhop(zz, hh, extra):
        return qhop_to(zz, hh, extra, s_qxe if extra else s_qx, across)

    def qphop(zz, hh, extra):
        index = owners + zz if extra else dp_of(zz, hh, c)
        return remote(qall.at[index], qall.at[index], s_qpassed, pqrecv.at[zz], dp=partner)

    qsigns = (turn, 1)

    def qbegin(extra):
        sign = qsigns[1 if extra else 0]
        qzhop(z, sign, extra).start()
        qzhop(z, -sign, extra).start()
        qxhop(z, h, extra).start()
        qphop(z, h, extra).start()

    def qhop(distance, extra=False):
        sign = qsigns[1 if extra else 0]
        for side, far in ((sign, 4), (-sign, 3)):
            if distance > far:
                continue
            zz = at(-side * distance)
            qxhop(zz, h, extra).wait_recv()
            if distance < far:
                qzhop(zz, side, extra).start()
            qxhop(zz, h, extra).start()
            qphop(zz, h, extra).start()

    def qacross(zz):
        qxhop(zz, 1 - h, False).wait_recv()
        qphop(zz, 1 - h, False).start()

        @pl.when(jnp.logical_and(on0, h == 1))
        def _():
            qxhop(zz, 0, True).wait_recv()
            qphop(zz, 0, True).start()

    def qstep(distance):
        qhop(distance)

        @pl.when(holder)
        def _():
            qhop(distance, True)

    def finish(js):
        results = polynomials([gall[j] for j in js], factor)
        for j, q in zip(js, results):
            qall[me if j == 0 else owners + z] = q.astype(BF16)
            qbegin(j == 1)
    strips(0, 1).wait_recv()
    @pl.when(holder)
    def _():
        strips(1, 1).wait_recv()
        finish((0, 1))

    @pl.when(jnp.logical_not(holder))
    def _():
        finish((0,))

    def both(distance):
        return (z,) if distance == 0 else (at(4),) if distance == 4 else (at(distance), at(-distance))

    def multiply(index):
        gathered[index] = dot(qall[index], nall[index]).astype(BF16)

    def apply(zz):
        for here, count in ((on0, 2), (on1, 3)):
            @pl.when(here)
            def _():
                several(nall.at[pl.ds(0, count)], s_passed, parecv.at[zz]).wait_recv()
                several(qall.at[pl.ds(0, count)], s_qpassed, pqrecv.at[zz]).wait_recv()

        for i in range(4):
            multiply(4 * zz + i)
        multiply(owners + zz)

    def crossing(distance):
        for zz in both(distance):
            from_across(zz)

    def qcrossing(distance):
        for zz in both(distance):
            qacross(zz)
    gather_step(1, (1,))
    gather_extra(1)
    hop(2, 2)
    crossing(0)
    crossing(1)
    qstep(1)
    gather_step(2, (0, 1))
    qcrossing(0)
    gather_extra(2)
    qstep(2)
    qcrossing(1)
    hop(2, 3)
    hop(0, 3)
    crossing(2)
    qstep(3)
    hop(1, 3)
    gather_extra(3)
    apply(z)
    hop(2, 4)
    crossing(3)
    qcrossing(2)
    qstep(4)
    for zz in both(1):
        apply(zz)
    gather_step(4, (0, 1))
    gather_extra(4)
    crossing(4)
    qcrossing(3)
    for zz in both(2):
        apply(zz)
    qcrossing(4)
    for zz in both(3):
        apply(zz)
    apply(at(4))
    has = jnp.float32(0.0)
    which = jnp.int32(0)
    for e in range(DEPTH):
        hit = table[HOLDER, e] == me
        has = jnp.where(hit, 1.0, has)
        which = jnp.where(hit, e, which)
    old = mv[1]
    mean = nall[owners + which].astype(F32) * (1.0 / GAIN) - (DECAY * DECAY / GAIN) * old
    new_momentum[0, 1] = old + has * ((DECAY * old + mean) - old)
    def left(ref, send):
        remote(ref, ref, send, zrecv_sem.at[0, 0], dp=across).wait_send()

    left(xstage, s_x)
    left(xstage, s_xbottom)
    left(xstage.at[0], s_xtop)
    left(qall.at[pl.ds(0, 7)], s_qz)
    left(qall.at[pl.ds(0, DEPTH)], s_qx)
    strips(0, 0).wait_send()
    strips(0, 1).wait_send()

    @pl.when(on1)
    def _():
        left(pstage, s_pair)
        left(zrecv.at[pl.ds(0, 3)], s_z)
        left(zrecv.at[pl.ds(0, 3)], s_az)
        left(tstage.at[0], s_top)
        left(nall.at[pl.ds(0, 16)], s_passed)
        left(qall.at[pl.ds(0, 16)], s_qpassed)

    @pl.when(on0)
    def _():
        left(pstage.at[pl.ds(0, 16)], s_pair)
        left(zrecv, s_z)
        left(zrecv, s_az)
        left(nall.at[pl.ds(0, 24)], s_passed)
        left(qall.at[pl.ds(0, 24)], s_qpassed)

        @pl.when(h == 1)
        def _():
            left(tstage, s_top)

        @pl.when(h == 0)
        def _():
            left(tstage.at[0], s_top)

    @pl.when(holder)
    def _():
        strips(1, 0).wait_send()
        strips(1, 1).wait_send()
        left(xstage.at[pl.ds(0, 2)], s_xextra)
        left(qall.at[pl.ds(0, 7)], s_qze)
        left(qall.at[pl.ds(0, DEPTH)], s_qxe)
def per_device(grads, owner, momentum):
    tensors = lax.axis_size("tensor")
    matrices, rows, cols = grads.shape[1:]
    slots = momentum.shape[1]
    half = rows // 2
    dma = pltpu.SemaphoreType.DMA
    whole = pl.BlockSpec(memory_space=pltpu.VMEM)
    far = pl.BlockSpec(memory_space=pltpu.HBM)
    gathered, new_momentum, table = pl.pallas_call(
        step_kernel,
        out_shape=(
            jax.ShapeDtypeStruct((matrices, rows, cols), BF16),
            jax.ShapeDtypeStruct(momentum.shape, F32),
            jax.ShapeDtypeStruct((8, 128), jnp.int32),
        ),
        in_specs=[far, far, far],
        out_specs=(whole, whole, whole),
        scratch_shapes=[
            pltpu.VMEM((matrices, rows, cols), BF16),
            pltpu.VMEM((slots, rows, cols), F32),
            pltpu.VMEM((24, rows, cols), BF16),
            pltpu.VMEM((24, rows, cols), BF16),
            pltpu.VMEM((DEPTH, half, cols), BF16),
            pltpu.VMEM((DEPTH, half, cols), BF16),
            pltpu.VMEM((5, 2, half, cols), BF16),
            pltpu.VMEM((5, 7, half, cols), BF16),
            pltpu.VMEM((3, half, cols), BF16),
            pltpu.VMEM((3, half, cols), BF16),
            pltpu.VMEM((2, rows, cols), F32),
            pltpu.VMEM((matrices, rows, cols), BF16),
            pltpu.VMEM((matrices, rows, rows), BF16),
            pltpu.VMEM((2, rows, rows), F32),
            pltpu.VMEM((2, tensors, rows // tensors, rows), F32),
            pltpu.VMEM((2, rows // tensors, rows), F32),
            pltpu.VMEM((2, rows, rows), F32),
            pltpu.SMEM((8, 128), jnp.int32),
            pltpu.VMEM((rows, cols), BF16),
            pltpu.VMEM((1, matrices), jnp.int32),
            dma((4,)), dma((18,)), dma((DEPTH,)), dma((DEPTH,)), dma((5, 7)), dma((2,)), dma((2, 2)),
            dma((6 * DEPTH,)), dma((DEPTH,)), dma((3 * DEPTH,)), dma((DEPTH,)),
        ],
        compiler_params=pltpu.CompilerParams(
            collective_id=0, has_side_effects=True, vmem_limit_bytes=46 * 2**20
        ),
        name="step",
    )(*(pltpu.with_memory_space_constraint(a, pltpu.HBM) for a in (owner.reshape(1, matrices), grads, momentum)))
    return pl.pallas_call(
        order_kernel,
        out_shape=(
            jax.ShapeDtypeStruct((matrices, rows, cols), BF16),
            jax.ShapeDtypeStruct(momentum.shape, F32),
        ),
        in_specs=[
            pl.BlockSpec(memory_space=pltpu.SMEM),
            pl.BlockSpec(memory_space=pl.ANY),
            pl.BlockSpec(memory_space=pl.ANY),
        ],
        out_specs=(far, far),
        scratch_shapes=[dma((matrices + 1,))],
        compiler_params=pltpu.CompilerParams(vmem_limit_bytes=2**20),
        name="order",
    )(table, gathered, new_momentum)


def solution(mesh):
    in_specs = (P("dp", None, None, "tensor"), P(), P("dp", None, None, "tensor"))
    out_specs = (P(None, None, "tensor"), P("dp", None, None, "tensor"))
    return jax.shard_map(
        per_device, mesh=mesh, in_specs=in_specs, out_specs=out_specs, check_vma=False
    )
```
